256 devices in a mesh: section: 16 (over z, y_lo), tile: 16 (over x, y_hi, core).
Axes of the slice: x: 4, y: 4 (y_hi: 2, y_lo: 2; y = y_hi * 2 + y_lo), z: 8, core: 2. Of those that a mesh axis runs over, the one named last changes fastest.
Arguments:
- acts: bfloat16 [16, 2, 256, 128, 128], P('section', None, None, 'tile'), may hold values from -6 to 6
- weights: bfloat16 [16, 9, 256, 256], P('section'), may hold values from -0.0625 to 0.0625
- cotangent: bfloat16 [2, 256, 128, 128], P(None, None, 'tile'), may hold values from -6 to 6
Outputs:
- grad_acts: bfloat16 [16, 2, 256, 128, 128], P('section', None, None, 'tile')
- weight_grad: float32 [16, 9, 256, 256], P('section')
The draws below stay inside these ranges and needn't reach their ends.
All inputs are finite; a program needn't handle non-finite values.
Results may differ from the reference program's by a relative error of at most 0.017.
Values may be sent and summed in bfloat16 or wider, within the bound.
No kernel may reach another device: no remote copies, remote signals or barrier semaphores. Data moves between devices by JAX's collectives and lax.ppermute only.
A program may use at most 64 MiB of HBM per device.

```python
import jax
import jax.numpy as jnp
from jax import lax

C = 256
MB = 2
COLS = 128
LAYERS = 16
ROWS = 128


def levels(key, extent, pieces, least, high):
    level, own = 1.0, jax.random.fold_in(key, 6)
    for position, blocks in pieces:
        draws = jnp.exp(jax.random.uniform(jax.random.fold_in(own, position), (blocks,), jnp.float32, least / len(pieces), high / len(pieces)))
        level = level * jnp.repeat(draws, extent[position] // blocks).reshape([-1 if axis == position else 1 for axis in range(len(extent))])
    return level


def normal_values(rng, extent, spread, most, shards=(), kind=jnp.bfloat16):
    array = spread * jax.random.normal(rng, extent, jnp.float32)
    if shards:
        array = array * levels(rng, extent, shards, -0.22, 0.18)
    return jnp.clip(array, -most, most).astype(kind)


def setup_inputs(seed: int = 0) -> dict:
    streams_of = jax.random.split(jax.random.key(seed), 4)
    acts = normal_values(streams_of[0], (LAYERS, MB, C, ROWS, COLS), 1.0, 6.0, ((0, 16), (3, 16)))
    weights = normal_values(streams_of[1], (LAYERS, 9, C, C), (36 * C) ** -0.5, 0.0625, ((0, 16),))
    cotangent = normal_values(streams_of[2], (MB, C, ROWS, COLS), 1.0, 6.0, ((2, 16),))
    return {"acts": acts, "weights": weights, "cotangent": cotangent}


def shift_cols(field, offset):
    if offset == 0:
        return field
    zeros = jnp.zeros_like(field[..., :1])
    if offset == 1:
        return jnp.concatenate([field[..., 1:], zeros], axis=-1)
    return jnp.concatenate([zeros, field[..., :-1]], axis=-1)

def reference(acts, weights, cotangent):
    scale = 1.0 / jnp.sqrt(jnp.float32(MB * ROWS * COLS))
    upper = cotangent
    grads = []
    kernels = []
    for layer in reversed(range(LAYERS)):
        inputs = acts[layer].astype(jnp.float32)
        sigma = jax.nn.sigmoid(inputs)
        hidden = (inputs * sigma).astype(jnp.bfloat16).astype(jnp.float32)
        slope = sigma * (1.0 + inputs * (1.0 - sigma))
        grad_up = upper.astype(jnp.float32)
        kernel = weights[layer].astype(jnp.float32)
        back = jnp.zeros_like(grad_up)
        parts = []
        for row_step in (-1, 0, 1):
            for col_step in (-1, 0, 1):
                index = (row_step + 1) * 3 + col_step + 1
                moved = shift_cols(jnp.roll(grad_up, row_step, axis=2), -col_step)
                back = back + jnp.einsum('oi,gorc->girc', kernel[index], moved, precision=lax.Precision.HIGHEST)
                seen = shift_cols(jnp.roll(hidden, -row_step, axis=2), col_step)
                parts.append(jnp.einsum('gorc,girc->oi', grad_up, seen, precision=lax.Precision.HIGHEST))
        kernels.append(jnp.stack(parts) * scale)
        upper = (grad_up + back * slope).astype(jnp.bfloat16)
        grads.append(upper)
    return (jnp.stack(grads[::-1]), jnp.stack(kernels[::-1]))
```

```python
import functools

import jax
import jax.numpy as jnp
from jax import lax
from jax.experimental import pallas as pl
from jax.experimental.pallas import tpu as pltpu
from jax.sharding import PartitionSpec as P

BOTH = ("section", "tile")
G = 4
C = 256
W = 128
BLK = 4
F32 = jnp.float32
BF16 = jnp.bfloat16


def route(target):
    pairs = []
    for s in range(16):
        for t in range(16):
            to = target(s, t)
            if to is not None:
                pairs.append((s * 16 + t, to[0] * 16 + to[1]))
    return pairs


def send(block, target):
    return lax.ppermute(block, BOTH, route(target))


def swap_member(block, d):
    return send(block, lambda s, t: (s ^ d, t))


def swap_core(block):
    return send(block, lambda s, t: (s, t ^ 1))


def col_masks(rows):
    lane = lax.broadcasted_iota(jnp.int32, (rows, W), 1)
    return lane == 0, lane == W - 1


def col_shifts(x, first, last):
    before = jnp.where(first, 0.0, pltpu.roll(x, 1, 1))
    after = jnp.where(last, 0.0, pltpu.roll(x, W - 1, 1))
    return before, after


def chain_kernel(ids, up, own, dn, w0, r1, r2, r3, c1, c2, c3, a0, a1, a2, a3,
                 out_p, out_g, out_last, wbuf, abuf, cat0, cat1, sem_w, sem_a):
    q = ids[0]
    core = ids[1]
    mine = pl.multiple_of(core * 128, 128)
    other = pl.multiple_of((1 - core) * 128, 128)
    halves = {1: (r1, c1), 2: (r2, c2), 3: (r3, c3)}
    pieces = (a0, a1, a2, a3)
    for layer in (3, 2, 1, 0):
        slot = q ^ layer
        for d in range(4):
            @pl.when(slot == d)
            def _(d=d, layer=layer):
                if d == 0:
                    pltpu.make_async_copy(w0, wbuf.at[layer], sem_w.at[layer]).start()
                else:
                    near, far = halves[d]
                    pltpu.make_async_copy(
                        near, wbuf.at[layer, pl.ds(mine, 128)], sem_w.at[layer]).start()
                    pltpu.make_async_copy(
                        far, wbuf.at[layer, pl.ds(other, 128)], sem_w.at[layer]).start()
                pltpu.make_async_copy(pieces[d], abuf.at[layer], sem_a.at[layer]).start()

    first, last = col_masks(C)

    def put(cat, row, x32):
        before, after = col_shifts(x32, first, last)
        lanes = slice(row * W, row * W + W)
        cat[0:C, lanes] = after.astype(BF16)
        cat[C:2 * C, lanes] = x32.astype(BF16)
        cat[2 * C:3 * C, lanes] = before.astype(BF16)

    for part, ref in enumerate((up, own, dn)):
        for r in range(BLK):
            put(cat0, part * BLK + r, ref[:, r * W:r * W + W].astype(F32))

    cats = (cat0, cat1)
    for j in range(4):
        layer = 3 - j
        slot = q ^ layer
        cur, nxt = cats[j % 2], cats[(j + 1) % 2]
        rows_out = 10 - 2 * j
        out_p[slot] = cur[C:2 * C, (4 - j) * W:(8 - j) * W]
        pltpu.make_async_copy(w0, wbuf.at[layer], sem_w.at[layer]).wait()
        pltpu.make_async_copy(a0, abuf.at[layer], sem_a.at[layer]).wait()
        for ch in range(rows_out // 2):
            back = None
            for a in (-1, 0, 1):
                start = (1 - a + 2 * ch) * W
                term = jnp.dot(
                    wbuf[layer, :, 768 * (a + 1):768 * (a + 2)],
                    cur[:, start:start + 2 * W],
                    preferred_element_type=F32,
                )
                back = term if back is None else back + term
            v = abuf[layer, :, (j + 2 * ch) * W:(j + 2 * ch + 2) * W].astype(F32)
            sig = 0.5 + 0.5 * jnp.tanh(0.5 * v)
            slope = sig * (1.0 + v * (1.0 - sig))
            mid = cur[C:2 * C, (1 + 2 * ch) * W:(3 + 2 * ch) * W].astype(F32)
            new = mid + back * slope
            if j < 3:
                put(nxt, 2 * ch, new[:, :W])
                put(nxt, 2 * ch + 1, new[:, W:])
            else:
                out_last[:, 2 * ch * W:(2 * ch + 2) * W] = new.astype(BF16)
        if j < 3:
            out_g[slot] = nxt[C:2 * C, (3 - j) * W:(7 - j) * W]
        else:
            out_g[slot] = out_last[...]


def chain(ids, up, own, dn, weights, pieces):
    vm = pl.BlockSpec(memory_space=pltpu.VMEM)
    hbm = pl.BlockSpec(memory_space=pl.ANY)
    n = BLK * W
    return pl.pallas_call(
        chain_kernel,
        out_shape=(
            jax.ShapeDtypeStruct((4, C, n), BF16),
            jax.ShapeDtypeStruct((4, C, n), BF16),
            jax.ShapeDtypeStruct((C, n), BF16),
        ),
        in_specs=[pl.BlockSpec(memory_space=pltpu.SMEM), vm, vm, vm] + [hbm] * 11,
        out_specs=(vm, vm, vm),
        scratch_shapes=[
            pltpu.VMEM((4, C, 9 * C), BF16),
            pltpu.VMEM((4, C, 10 * W), BF16),
            pltpu.VMEM((3 * C, 12 * W), BF16),
            pltpu.VMEM((3 * C, 12 * W), BF16),
            pltpu.SemaphoreType.DMA((4,)),
            pltpu.SemaphoreType.DMA((4,)),
        ],
        compiler_params=pltpu.CompilerParams(vmem_limit_bytes=40 << 20),
        cost_estimate=pl.CostEstimate(
            flops=2 * 9 * C * C * 28 * W, bytes_accessed=10 << 20, transcendentals=28 * W * C),
        name="chain",
    )(ids, up, own, dn, *weights, *pieces)


def hidden_kernel(a_ref, h_ref):
    first, last = col_masks(C)
    for r in range(10):
        lanes = slice(r * W, r * W + W)
        v = a_ref[0, :, lanes].astype(F32)
        hid = v * (0.5 + 0.5 * jnp.tanh(0.5 * v))
        before, after = col_shifts(hid, first, last)
        h_ref[0, 0:C, lanes] = before.astype(BF16)
        h_ref[0, C:2 * C, lanes] = hid.astype(BF16)
        h_ref[0, 2 * C:3 * C, lanes] = after.astype(BF16)


def hidden_shifts(acts_rim):
    return pl.pallas_call(
        hidden_kernel,
        grid=(2,),
        out_shape=jax.ShapeDtypeStruct((2, 3 * C, 10 * W), BF16),
        in_specs=[pl.BlockSpec((1, C, 10 * W), lambda b: (b, 0, 0))],
        out_specs=pl.BlockSpec((1, 3 * C, 10 * W), lambda b: (b, 0, 0)),
        compiler_params=pltpu.CompilerParams(vmem_limit_bytes=40 << 20),
        cost_estimate=pl.CostEstimate(
            flops=10 * 2 * C * 10 * W, bytes_accessed=6 << 20, transcendentals=2 * C * 10 * W),
        name="hidden",
    )(acts_rim)


def wgrad_kernel(scale, ids, p0, p1, p2, p3, h_ref, out, upper):
    q = ids[0]
    for d, ref in enumerate((p0, p1, p2, p3)):
        pos = q ^ d
        half = pl.multiple_of((pos & 1) * (BLK * W), BLK * W)
        upper[pos >> 1, :, pl.ds(half, BLK * W)] = ref[...]
    for a in (-1, 0, 1):
        acc = None
        for b in range(2):
            term = lax.dot_general(
                upper[b], h_ref[b, :, (1 + a) * W:(9 + a) * W],
                (((1,), (1,)), ((), ())), preferred_element_type=F32)
            acc = term if acc is None else acc + term
        acc = (acc * scale).astype(BF16)
        for b in range(3):
            for piece in range(16):
                out[piece // 8, piece % 8, 3 * (a + 1) + b] = (
                    acc[piece * 16:piece * 16 + 16, b * C:b * C + C])


def wgrad(scale, ids, parts, hid):
    vm = pl.BlockSpec(memory_space=pltpu.VMEM)
    return pl.pallas_call(
        functools.partial(wgrad_kernel, scale),
        out_shape=jax.ShapeDtypeStruct((2, 8, 9, 16, C), BF16),
        in_specs=[pl.BlockSpec(memory_space=pltpu.SMEM)] + [vm] * 5,
        out_specs=vm,
        scratch_shapes=[pltpu.VMEM((2, C, 8 * W), BF16)],
        compiler_params=pltpu.CompilerParams(vmem_limit_bytes=40 << 20),
        cost_estimate=pl.CostEstimate(
            flops=2 * 9 * C * C * 2048, bytes_accessed=6 << 20, transcendentals=0),
        name="wgrad",
    )(ids, *parts, hid)


def place_kernel(ids, g0, g1, g2, g3, out):
    q = ids[0]
    for d, ref in enumerate((g0, g1, g2, g3)):
        pos = q ^ d
        half = pl.multiple_of((pos & 1) * (BLK * W), BLK * W)
        out[pos >> 1, :, pl.ds(half, BLK * W)] = ref[...]


def place(ids, parts):
    vm = pl.BlockSpec(memory_space=pltpu.VMEM)
    return pl.pallas_call(
        place_kernel,
        out_shape=jax.ShapeDtypeStruct((2, C, 8 * W), BF16),
        in_specs=[pl.BlockSpec(memory_space=pltpu.SMEM)] + [vm] * 4,
        out_specs=vm,
        cost_estimate=pl.CostEstimate(flops=0, bytes_accessed=2 << 20, transcendentals=0),
        name="place",
    )(ids, *parts)


def unpack_kernel(ids, near, far, out):
    core = ids[1]
    chip = ids[2]
    for e in range(8):
        piece = chip ^ e
        for side, ref in ((core, near), (1 - core, far)):
            row = pl.multiple_of(side * 128 + piece * 16, 16)
            out[:, pl.ds(row, 16), :] = ref[e].astype(F32)


def unpack(ids, near, far):
    vm = pl.BlockSpec(memory_space=pltpu.VMEM)
    return pl.pallas_call(
        unpack_kernel,
        out_shape=jax.ShapeDtypeStruct((9, C, C), F32),
        in_specs=[pl.BlockSpec(memory_space=pltpu.SMEM)] + [vm] * 2,
        out_specs=vm,
        cost_estimate=pl.CostEstimate(flops=0, bytes_accessed=4 << 20, transcendentals=0),
        name="unpack",
    )(ids, near, far)


def per_device(acts, weights, cotangent):
    section = lax.axis_index("section")
    tile = lax.axis_index("tile")
    q = section & 3
    group = section >> 2
    core = tile & 1
    chip = tile >> 1
    ids = jnp.stack([q, core, chip]).astype(jnp.int32)
    n = BLK * W

    wt = weights[0].transpose(2, 0, 1).reshape(C, 9 * C)
    w_half = lax.dynamic_slice(wt, (core * 128, 0), (128, 9 * C))
    near = [swap_member(w_half, d) for d in (1, 2, 3)]
    far = [swap_core(block) for block in near]
    slots = [wt] + near + far

    flat = acts[0].reshape(2, C, 8 * W)
    low = send(flat[:, :, 5 * W:], lambda s, t: (s, (t + 1) % 16))
    high = send(flat[:, :, :3 * W], lambda s, t: (s, (t - 1) % 16))
    ext = jnp.concatenate([low, flat, high], axis=2)

    def piece_of(member):
        return lax.dynamic_slice(
            ext, (member >> 1, 0, (member & 1) * n), (1, C, 10 * W))[0]

    pieces = [piece_of(q)] + [swap_member(piece_of(q ^ d), d) for d in (1, 2, 3)]
    hid = hidden_shifts(ext[:, :, 2 * W:12 * W])

    own = lax.dynamic_slice(
        cotangent, (q >> 1, 0, (q & 1) * BLK, 0), (1, C, BLK, W)).reshape(C, n)
    last = own
    for tick in range(4):
        if tick:
            got = send(last, lambda s, t: (s - 4, t) if s >> 2 == 4 - tick else None)
            own = jnp.where(group == 3 - tick, got, own)
        up = send(own, lambda s, t: (s ^ 1, t) if s & 1 == 0 else (s ^ 1, (t + 1) % 16))
        dn = send(own, lambda s, t: (s ^ 1, t) if s & 1 == 1 else (s ^ 1, (t - 1) % 16))
        out_p, out_g, last = chain(ids, up, own, dn, slots, pieces)

    parts = [out_p[0]] + [swap_member(out_p[d], d) for d in (1, 2, 3)]
    grads = [out_g[0]] + [swap_member(out_g[d], d) for d in (1, 2, 3)]

    scale = 1.0 / (2 * 128 * 128) ** 0.5
    partial = wgrad(scale, ids, parts, hid)
    kept = lax.dynamic_index_in_dim(partial, core, 0, keepdims=False).astype(F32)
    given = swap_core(lax.dynamic_index_in_dim(partial, 1 - core, 0, keepdims=False))
    both = kept + given.astype(F32)
    total = lax.dynamic_index_in_dim(both, chip, 0, keepdims=False)
    both16 = both.astype(BF16)
    for e in range(1, 8):
        block = lax.dynamic_index_in_dim(both16, chip ^ e, 0, keepdims=False)
        total = total + send(block, lambda s, t: (s, t ^ (2 * e))).astype(F32)
    total = total.astype(BF16)
    gathered = jnp.stack(
        [total] + [send(total, lambda s, t: (s, t ^ (2 * e))) for e in range(1, 8)])
    weight_grad = unpack(ids, gathered, swap_core(gathered))

    grad_acts = place(ids, grads).reshape(1, 2, C, 8, W)
    return (grad_acts, weight_grad[None])


def solution(mesh):
    placed = (
        P("section", None, None, "tile", None),
        P("section", None, None, None),
        P(None, None, "tile", None),
    )
    return jax.shard_map(
        per_device,
        mesh=mesh,
        in_specs=placed,
        out_specs=(P("section", None, None, "tile", None), P("section", None, None, None)),
        check_vma=False,
    )
```

```python
import functools

import jax
import jax.numpy as jnp
from jax import lax
from jax.experimental import pallas as pl
from jax.experimental.pallas import tpu as pltpu
from jax.sharding import Mesh, PartitionSpec as P

SECTION = "section"
TILE = ("x", "yhi", "core")
BOTH = (SECTION,) + TILE
C = 256
W = 128
BLK = 4
F32 = jnp.float32
BF16 = jnp.bfloat16


def route(target):
    pairs = []
    for s in range(16):
        for t in range(16):
            to = target(s, t)
            if to is not None:
                pairs.append((s * 16 + t, to[0] * 16 + to[1]))
    return pairs


def send(block, target):
    return lax.ppermute(block, BOTH, route(target))


def swap_member(block, d):
    return send(block, lambda s, t: (s ^ d, t))


def swap_core(block):
    return send(block, lambda s, t: (s, t ^ 1))


def from_above(block):
    return send(block, lambda s, t: (s ^ 1, t if s & 1 == 0 else (t + 1) % 16))


def from_below(block):
    return send(block, lambda s, t: (s ^ 1, t if s & 1 == 1 else (t - 1) % 16))


def col_masks(rows):
    lane = lax.broadcasted_iota(jnp.int32, (rows, W), 1)
    return lane == 0, lane == W - 1


def col_shifts(x, first, last):
    before = jnp.where(first, 0.0, pltpu.roll(x, 1, 1))
    after = jnp.where(last, 0.0, pltpu.roll(x, W - 1, 1))
    return before, after


def pack_kernel(ids, p0, p1, p2, p3, own, top, bottom):
    q = ids[0]
    at = {3: 0, 2: 3, 1: 5}
    for layer in range(4):
        for d, ref in enumerate((p0, p1, p2, p3)):
            @pl.when((q ^ d) == layer)
            def _(layer=layer, ref=ref):
                own[layer] = ref[...]
                if layer:
                    lanes = slice(at[layer] * W, (at[layer] + layer) * W)
                    top[:, lanes] = ref[:, :layer * W]
                    bottom[:, lanes] = ref[:, (BLK - layer) * W:]


def pack(ids, pieces):
    vm = pl.BlockSpec(memory_space=pltpu.VMEM)
    return pl.pallas_call(
        pack_kernel,
        out_shape=(
            jax.ShapeDtypeStruct((4, C, BLK * W), BF16),
            jax.ShapeDtypeStruct((C, 6 * W), BF16),
            jax.ShapeDtypeStruct((C, 6 * W), BF16),
        ),
        in_specs=[pl.BlockSpec(memory_space=pltpu.SMEM)] + [vm] * 4,
        out_specs=(vm, vm, vm),
        cost_estimate=pl.CostEstimate(flops=0, bytes_accessed=3 << 20, transcendentals=0),
        name="pack",
    )(ids, *pieces)


def chain_kernel(ids, up, own, dn, w0, r1, r2, r3, c1, c2, c3, a_own, a_up, a_dn,
                 out_p, out_g, out_last, wbuf, vown, vup, vdn, cat0, cat1, sem_w, sem_a):
    q = ids[0]
    core = ids[1]
    mine = pl.multiple_of(core * 128, 128)
    other = pl.multiple_of((1 - core) * 128, 128)
    halves = {1: (r1, c1), 2: (r2, c2), 3: (r3, c3)}
    stored = [
        pltpu.make_async_copy(a_own, vown, sem_a.at[0]),
        pltpu.make_async_copy(a_up, vup, sem_a.at[1]),
        pltpu.make_async_copy(a_dn, vdn, sem_a.at[2]),
    ]
    for layer in (3, 2, 1, 0):
        slot = q ^ layer
        for d in range(4):
            @pl.when(slot == d)
            def _(d=d, layer=layer):
                if d == 0:
                    pltpu.make_async_copy(w0, wbuf.at[layer], sem_w.at[layer]).start()
                else:
                    near, far = halves[d]
                    pltpu.make_async_copy(
                        near, wbuf.at[layer, pl.ds(mine, 128)], sem_w.at[layer]).start()
                    pltpu.make_async_copy(
                        far, wbuf.at[layer, pl.ds(other, 128)], sem_w.at[layer]).start()
        if layer == 3:
            for copy in stored:
                copy.start()

    first, last = col_masks(C)

    def put(cat, row, x32):
        before, after = col_shifts(x32, first, last)
        lanes = slice(row * W, row * W + W)
        cat[0:C, lanes] = after.astype(BF16)
        cat[C:2 * C, lanes] = x32.astype(BF16)
        cat[2 * C:3 * C, lanes] = before.astype(BF16)

    for part, ref in enumerate((up, own, dn)):
        for r in range(BLK):
            put(cat0, part * BLK + r, ref[:, r * W:r * W + W].astype(F32))
    for copy in stored:
        copy.wait()

    at = {3: 0, 2: 3, 1: 5}

    def stored_row(layer, r):
        if r < layer:
            ref, row = vup, at[layer] + r
        elif r < layer + BLK:
            return vown[layer, :, (r - layer) * W:(r - layer + 1) * W].astype(F32)
        else:
            ref, row = vdn, at[layer] + r - layer - BLK
        return ref[:, row * W:row * W + W].astype(F32)

    cats = (cat0, cat1)
    for j in range(4):
        layer = 3 - j
        slot = q ^ layer
        cur, nxt = cats[j % 2], cats[(j + 1) % 2]
        rows_out = 10 - 2 * j
        out_p[slot] = cur[C:2 * C, (4 - j) * W:(8 - j) * W]
        pltpu.make_async_copy(w0, wbuf.at[layer], sem_w.at[layer]).wait()
        for ch in range(rows_out // 2):
            back = None
            for a in (-1, 0, 1):
                start = (1 - a + 2 * ch) * W
                term = jnp.dot(
                    wbuf[layer, :, 768 * (a + 1):768 * (a + 2)],
                    cur[:, start:start + 2 * W],
                    preferred_element_type=F32,
                )
                back = term if back is None else back + term
            for r in (2 * ch, 2 * ch + 1):
                v = stored_row(layer, r)
                sig = 0.5 + 0.5 * jnp.tanh(0.5 * v)
                slope = sig * (1.0 + v * (1.0 - sig))
                mid = cur[C:2 * C, (1 + r) * W:(2 + r) * W].astype(F32)
                new = mid + back[:, (r - 2 * ch) * W:(r - 2 * ch + 1) * W] * slope
                if j < 3:
                    put(nxt, r, new)
                else:
                    out_last[:, r * W:r * W + W] = new.astype(BF16)
        if j < 3:
            out_g[slot] = nxt[C:2 * C, (3 - j) * W:(7 - j) * W]
        else:
            out_g[slot] = out_last[...]


def chain(ids, up, own, dn, weights, stored):
    vm = pl.BlockSpec(memory_space=pltpu.VMEM)
    hbm = pl.BlockSpec(memory_space=pl.ANY)
    n = BLK * W
    return pl.pallas_call(
        chain_kernel,
        out_shape=(
            jax.ShapeDtypeStruct((4, C, n), BF16),
            jax.ShapeDtypeStruct((4, C, n), BF16),
            jax.ShapeDtypeStruct((C, n), BF16),
        ),
        in_specs=[pl.BlockSpec(memory_space=pltpu.SMEM), vm, vm, vm] + [hbm] * 10,
        out_specs=(vm, vm, vm),
        scratch_shapes=[
            pltpu.VMEM((4, C, 9 * C), BF16),
            pltpu.VMEM((4, C, n), BF16),
            pltpu.VMEM((C, 6 * W), BF16),
            pltpu.VMEM((C, 6 * W), BF16),
            pltpu.VMEM((3 * C, 12 * W), BF16),
            pltpu.VMEM((3 * C, 12 * W), BF16),
            pltpu.SemaphoreType.DMA((4,)),
            pltpu.SemaphoreType.DMA((3,)),
        ],
        compiler_params=pltpu.CompilerParams(vmem_limit_bytes=40 << 20),
        cost_estimate=pl.CostEstimate(
            flops=2 * 9 * C * C * 28 * W, bytes_accessed=10 << 20, transcendentals=28 * W * C),
        name="chain",
    )(ids, up, own, dn, *weights, *stored)


def hidden_kernel(a_ref, h_ref):
    first, last = col_masks(C)
    for r in range(10):
        lanes = slice(r * W, r * W + W)
        v = a_ref[0, :, lanes].astype(F32)
        hid = v * (0.5 + 0.5 * jnp.tanh(0.5 * v))
        before, after = col_shifts(hid, first, last)
        h_ref[0, 0:C, lanes] = before.astype(BF16)
        h_ref[0, C:2 * C, lanes] = hid.astype(BF16)
        h_ref[0, 2 * C:3 * C, lanes] = after.astype(BF16)


def hidden_shifts(acts_rim):
    return pl.pallas_call(
        hidden_kernel,
        grid=(2,),
        out_shape=jax.ShapeDtypeStruct((2, 3 * C, 10 * W), BF16),
        in_specs=[pl.BlockSpec((1, C, 10 * W), lambda b: (b, 0, 0))],
        out_specs=pl.BlockSpec((1, 3 * C, 10 * W), lambda b: (b, 0, 0)),
        compiler_params=pltpu.CompilerParams(vmem_limit_bytes=40 << 20),
        cost_estimate=pl.CostEstimate(
            flops=10 * 2 * C * 10 * W, bytes_accessed=6 << 20, transcendentals=2 * C * 10 * W),
        name="hidden",
    )(acts_rim)


def wgrad_kernel(scale, ids, p0, p1, p2, p3, h_hbm, out, upper, hid, sem):
    q = ids[0]
    copies = [pltpu.make_async_copy(h_hbm.at[b], hid.at[b], sem.at[b]) for b in range(2)]
    for d, ref in enumerate((p0, p1, p2, p3)):
        pos = q ^ d
        half = pl.multiple_of((pos & 1) * (BLK * W), BLK * W)
        copies.append(pltpu.make_async_copy(
            ref, upper.at[pos >> 1, :, pl.ds(half, BLK * W)], sem.at[2 + d]))
    for copy in copies:
        copy.start()
    for copy in copies:
        copy.wait()
    for a in (-1, 0, 1):
        acc = None
        for b in range(2):
            term = lax.dot_general(
                upper[b], hid[b, :, (1 + a) * W:(9 + a) * W],
                (((1,), (1,)), ((), ())), preferred_element_type=F32)
            acc = term if acc is None else acc + term
        acc = (acc * scale).astype(BF16)
        for b in range(3):
            for piece in range(16):
                out[piece, 3 * (a + 1) + b] = acc[piece * 16:piece * 16 + 16, b * C:b * C + C]


def wgrad(scale, ids, parts, hid):
    hbm = pl.BlockSpec(memory_space=pl.ANY)
    return pl.pallas_call(
        functools.partial(wgrad_kernel, scale),
        out_shape=jax.ShapeDtypeStruct((16, 9, 16, C), BF16),
        in_specs=[pl.BlockSpec(memory_space=pltpu.SMEM)] + [hbm] * 5,
        out_specs=pl.BlockSpec(memory_space=pltpu.VMEM),
        scratch_shapes=[
            pltpu.VMEM((2, C, 8 * W), BF16),
            pltpu.VMEM((2, 3 * C, 10 * W), BF16),
            pltpu.SemaphoreType.DMA((6,)),
        ],
        compiler_params=pltpu.CompilerParams(vmem_limit_bytes=40 << 20),
        cost_estimate=pl.CostEstimate(
            flops=2 * 9 * C * C * 2048, bytes_accessed=6 << 20, transcendentals=0),
        name="wgrad",
    )(ids, *parts, hid)


def place_kernel(ids, g0, g1, g2, g3, out):
    q = ids[0]
    for d, ref in enumerate((g0, g1, g2, g3)):
        pos = q ^ d
        half = pl.multiple_of((pos & 1) * (BLK * W), BLK * W)
        out[pos >> 1, :, pl.ds(half, BLK * W)] = ref[...]


def place(ids, parts):
    vm = pl.BlockSpec(memory_space=pltpu.VMEM)
    return pl.pallas_call(
        place_kernel,
        out_shape=jax.ShapeDtypeStruct((2, C, 8 * W), BF16),
        in_specs=[pl.BlockSpec(memory_space=pltpu.SMEM)] + [vm] * 4,
        out_specs=vm,
        cost_estimate=pl.CostEstimate(flops=0, bytes_accessed=2 << 20, transcendentals=0),
        name="place",
    )(ids, *parts)


def unpack_kernel(ids, near, far, out):
    core = ids[1]
    for chip in range(8):
        for side, ref in ((core, near), (1 - core, far)):
            row = pl.multiple_of(chip * 32 + side * 16, 16)
            out[:, pl.ds(row, 16), :] = ref[chip].astype(F32)


def unpack(ids, near, far):
    vm = pl.BlockSpec(memory_space=pltpu.VMEM)
    return pl.pallas_call(
        unpack_kernel,
        out_shape=jax.ShapeDtypeStruct((9, C, C), F32),
        in_specs=[pl.BlockSpec(memory_space=pltpu.SMEM)] + [vm] * 2,
        out_specs=vm,
        cost_estimate=pl.CostEstimate(flops=0, bytes_accessed=4 << 20, transcendentals=0),
        name="unpack",
    )(ids, near, far)


def per_device(acts, weights, cotangent):
    section = lax.axis_index(SECTION)
    tile = lax.axis_index(TILE)
    q = section & 3
    group = section >> 2
    core = tile & 1
    ids = jnp.stack([q, core]).astype(jnp.int32)
    n = BLK * W

    cot = lax.dynamic_slice(
        cotangent, (q >> 1, 0, (q & 1) * BLK, 0), (1, C, BLK, W)).reshape(C, n)

    wt = weights[0].transpose(2, 0, 1).reshape(C, 9 * C)
    w_half = lax.dynamic_slice(wt, (core * 128, 0), (128, 9 * C))
    flat = acts[0].reshape(2, C, 8 * W)

    def piece_of(member):
        return lax.dynamic_slice(flat, (member >> 1, 0, (member & 1) * n), (1, C, n))[0]

    near_y = swap_member(w_half, 1)
    near_z = swap_member(w_half, 2)
    pieces = [piece_of(q)] + [swap_member(piece_of(q ^ d), d) for d in (1, 2, 3)]
    near_d = swap_member(near_y, 2)
    near = [near_y, near_z, near_d]
    slots = [wt] + near + [swap_core(block) for block in near]
    a_own, top, bottom = pack(ids, pieces)
    stored = (a_own, from_above(bottom), from_below(top))

    own = last = cot
    for tick in range(4):
        if tick:
            got = send(last, lambda s, t: (s - 4, t) if s >> 2 == 4 - tick else None)
            own = jnp.where(group == 3 - tick, got, own)
        if tick == 1:
            low = send(flat[:, :, 7 * W:], lambda s, t: (s, (t + 1) % 16))
            high = send(flat[:, :, :W], lambda s, t: (s, (t - 1) % 16))
            hid = hidden_shifts(jnp.concatenate([low, flat, high], axis=2))
        if tick == 3:
            own, hid = lax.optimization_barrier((own, hid))
        out_p, out_g, last = chain(ids, from_above(own), own, from_below(own), slots, stored)

    parts = [out_p[0]] + [swap_member(out_p[d], d) for d in (1, 2, 3)]
    grads = [out_g[0]] + [swap_member(out_g[d], d) for d in (1, 2, 3)]

    scale = 1.0 / (2 * 128 * 128) ** 0.5
    partial = wgrad(scale, ids, parts, hid)
    partial, grads = lax.optimization_barrier((partial, grads))
    pieces = lax.all_to_all(partial, TILE, 0, 0, tiled=True)
    total = jnp.sum(pieces.astype(F32), axis=0).astype(BF16)
    copies = jnp.broadcast_to(total[None], (8,) + total.shape)
    gathered = lax.all_to_all(copies, ("x", "yhi"), 0, 0, tiled=True)
    weight_grad = unpack(ids, gathered, swap_core(gathered))

    grad_acts = place(ids, grads).reshape(1, 2, C, 8, W)
    return (grad_acts, weight_grad[None])


def solution(mesh):
    fine = Mesh(mesh.devices.reshape(16, 4, 2, 2), ("section", "x", "yhi", "core"))
    placed = (
        P(SECTION, None, None, TILE, None),
        P(SECTION, None, None, None),
        P(None, None, TILE, None),
    )
    return jax.shard_map(
        per_device,
        mesh=fine,
        in_specs=placed,
        out_specs=(P(SECTION, None, None, TILE, None), P(SECTION, None, None, None)),
        check_vma=False,
    )
```

```python
import functools

import jax
import jax.numpy as jnp
from jax import lax
from jax.experimental import pallas as pl
from jax.experimental.pallas import tpu as pltpu
from jax.sharding import Mesh, PartitionSpec as P

SECTION = "section"
TILE = ("x", "yhi", "core")
BOTH = (SECTION,) + TILE
C = 256
W = 128
BLK = 4
F32 = jnp.float32
BF16 = jnp.bfloat16


def route(target):
    pairs = []
    for s in range(16):
        for t in range(16):
            to = target(s, t)
            if to is not None:
                pairs.append((s * 16 + t, to[0] * 16 + to[1]))
    return pairs


def send(block, target):
    return lax.ppermute(block, BOTH, route(target))


def swap_member(block, d):
    return send(block, lambda s, t: (s ^ d, t))


def swap_core(block):
    return send(block, lambda s, t: (s, t ^ 1))


def from_above(block):
    return send(block, lambda s, t: (s ^ 1, t if s & 1 == 0 else (t + 1) % 16))


def from_below(block):
    return send(block, lambda s, t: (s ^ 1, t if s & 1 == 1 else (t - 1) % 16))


def col_masks(rows):
    lane = lax.broadcasted_iota(jnp.int32, (rows, W), 1)
    return lane == 0, lane == W - 1


def col_shifts(x, first, last):
    before = jnp.where(first, 0.0, pltpu.roll(x, 1, 1))
    after = jnp.where(last, 0.0, pltpu.roll(x, W - 1, 1))
    return before, after


def in_hbm(x):
    return pltpu.with_memory_space_constraint(x, pltpu.HBM)


def pack_kernel(ids, p0, p1, p2, p3, own, top, bottom):
    q = ids[0]
    at = {3: 0, 2: 3, 1: 5}
    for layer in range(4):
        for d, ref in enumerate((p0, p1, p2, p3)):
            @pl.when((q ^ d) == layer)
            def _(layer=layer, ref=ref):
                own[layer] = ref[...]
                if layer:
                    lanes = slice(at[layer] * W, (at[layer] + layer) * W)
                    top[:, lanes] = ref[:, :layer * W]
                    bottom[:, lanes] = ref[:, (BLK - layer) * W:]


def pack(ids, pieces):
    vm = pl.BlockSpec(memory_space=pltpu.VMEM)
    return pl.pallas_call(
        pack_kernel,
        out_shape=(
            jax.ShapeDtypeStruct((4, C, BLK * W), BF16),
            jax.ShapeDtypeStruct((C, 6 * W), BF16),
            jax.ShapeDtypeStruct((C, 6 * W), BF16),
        ),
        in_specs=[pl.BlockSpec(memory_space=pltpu.SMEM)] + [vm] * 4,
        out_specs=(vm, vm, vm),
        cost_estimate=pl.CostEstimate(flops=0, bytes_accessed=3 << 20, transcendentals=0),
        name="pack",
    )(ids, *pieces)


def chain_kernel(ids, up, own, dn, w0, r1, r2, r3, c1, c2, c3, a_own, a_up, a_dn,
                 out_p, out_g, out_last, wbuf, vown, vup, vdn, cat0, cat1, sem_w, sem_a):
    q = ids[0]
    core = ids[1]
    mine = pl.multiple_of(core * 128, 128)
    other = pl.multiple_of((1 - core) * 128, 128)
    halves = {1: (r1, c1), 2: (r2, c2), 3: (r3, c3)}
    stored = [
        pltpu.make_async_copy(a_own, vown, sem_a.at[0]),
        pltpu.make_async_copy(a_up, vup, sem_a.at[1]),
        pltpu.make_async_copy(a_dn, vdn, sem_a.at[2]),
    ]
    for layer in (3, 2, 1, 0):
        slot = q ^ layer
        for d in range(4):
            @pl.when(slot == d)
            def _(d=d, layer=layer):
                if d == 0:
                    pltpu.make_async_copy(w0, wbuf.at[layer], sem_w.at[layer]).start()
                else:
                    near, far = halves[d]
                    pltpu.make_async_copy(
                        near, wbuf.at[layer, pl.ds(mine, 128)], sem_w.at[layer]).start()
                    pltpu.make_async_copy(
                        far, wbuf.at[layer, pl.ds(other, 128)], sem_w.at[layer]).start()
        if layer == 3:
            for copy in stored:
                copy.start()

    first, last = col_masks(C)

    def put(cat, row, x32):
        before, after = col_shifts(x32, first, last)
        lanes = slice(row * W, row * W + W)
        cat[0:C, lanes] = after.astype(BF16)
        cat[C:2 * C, lanes] = x32.astype(BF16)
        cat[2 * C:3 * C, lanes] = before.astype(BF16)

    for part, ref in enumerate((up, own, dn)):
        for r in range(BLK):
            put(cat0, part * BLK + r, ref[:, r * W:r * W + W].astype(F32))
    for copy in stored:
        copy.wait()

    at = {3: 0, 2: 3, 1: 5}

    def stored_row(layer, r):
        if r < layer:
            ref, row = vup, at[layer] + r
        elif r < layer + BLK:
            return vown[layer, :, (r - layer) * W:(r - layer + 1) * W].astype(F32)
        else:
            ref, row = vdn, at[layer] + r - layer - BLK
        return ref[:, row * W:row * W + W].astype(F32)

    cats = (cat0, cat1)
    for j in range(4):
        layer = 3 - j
        slot = q ^ layer
        cur, nxt = cats[j % 2], cats[(j + 1) % 2]
        rows_out = 10 - 2 * j
        out_p[slot] = cur[C:2 * C, (4 - j) * W:(8 - j) * W]
        pltpu.make_async_copy(w0, wbuf.at[layer], sem_w.at[layer]).wait()
        for ch in range(rows_out // 2):
            back = None
            for a in (-1, 0, 1):
                start = (1 - a + 2 * ch) * W
                term = jnp.dot(
                    wbuf[layer, :, 768 * (a + 1):768 * (a + 2)],
                    cur[:, start:start + 2 * W],
                    preferred_element_type=F32,
                )
                back = term if back is None else back + term
            for r in (2 * ch, 2 * ch + 1):
                v = stored_row(layer, r)
                sig = 0.5 + 0.5 * jnp.tanh(0.5 * v)
                slope = sig * (1.0 + v * (1.0 - sig))
                mid = cur[C:2 * C, (1 + r) * W:(2 + r) * W].astype(F32)
                new = mid + back[:, (r - 2 * ch) * W:(r - 2 * ch + 1) * W] * slope
                if j < 3:
                    put(nxt, r, new)
                else:
                    out_last[:, r * W:r * W + W] = new.astype(BF16)
        if j < 3:
            out_g[slot] = nxt[C:2 * C, (3 - j) * W:(7 - j) * W]
        else:
            out_g[slot] = out_last[...]


def chain(ids, up, own, dn, weights, stored):
    vm = pl.BlockSpec(memory_space=pltpu.VMEM)
    hbm = pl.BlockSpec(memory_space=pl.ANY)
    n = BLK * W
    return pl.pallas_call(
        chain_kernel,
        out_shape=(
            jax.ShapeDtypeStruct((4, C, n), BF16),
            jax.ShapeDtypeStruct((4, C, n), BF16),
            jax.ShapeDtypeStruct((C, n), BF16),
        ),
        in_specs=[pl.BlockSpec(memory_space=pltpu.SMEM), vm, vm, vm] + [hbm] * 10,
        out_specs=(vm, vm, vm),
        scratch_shapes=[
            pltpu.VMEM((4, C, 9 * C), BF16),
            pltpu.VMEM((4, C, n), BF16),
            pltpu.VMEM((C, 6 * W), BF16),
            pltpu.VMEM((C, 6 * W), BF16),
            pltpu.VMEM((3 * C, 12 * W), BF16),
            pltpu.VMEM((3 * C, 12 * W), BF16),
            pltpu.SemaphoreType.DMA((4,)),
            pltpu.SemaphoreType.DMA((3,)),
        ],
        compiler_params=pltpu.CompilerParams(vmem_limit_bytes=40 << 20),
        cost_estimate=pl.CostEstimate(
            flops=2 * 9 * C * C * 28 * W, bytes_accessed=10 << 20, transcendentals=28 * W * C),
        name="chain",
    )(ids, up, own, dn, *[in_hbm(x) for x in (*weights, *stored)])


def hidden_kernel(a_ref, h_ref):
    first, last = col_masks(C)
    for r in range(10):
        lanes = slice(r * W, r * W + W)
        v = a_ref[0, :, lanes].astype(F32)
        hid = v * (0.5 + 0.5 * jnp.tanh(0.5 * v))
        before, after = col_shifts(hid, first, last)
        h_ref[0, 0:C, lanes] = before.astype(BF16)
        h_ref[0, C:2 * C, lanes] = hid.astype(BF16)
        h_ref[0, 2 * C:3 * C, lanes] = after.astype(BF16)


def hidden_shifts(acts_rim):
    return pl.pallas_call(
        hidden_kernel,
        grid=(2,),
        out_shape=jax.ShapeDtypeStruct((2, 3 * C, 10 * W), BF16),
        in_specs=[pl.BlockSpec((1, C, 10 * W), lambda b: (b, 0, 0))],
        out_specs=pl.BlockSpec((1, 3 * C, 10 * W), lambda b: (b, 0, 0)),
        compiler_params=pltpu.CompilerParams(vmem_limit_bytes=40 << 20),
        cost_estimate=pl.CostEstimate(
            flops=10 * 2 * C * 10 * W, bytes_accessed=6 << 20, transcendentals=2 * C * 10 * W),
        name="hidden",
    )(acts_rim)


def wgrad_kernel(scale, ids, p0, p1, p2, p3, h_hbm, keep, give, upper, hid, sem):
    q = ids[0]
    core = ids[1]
    copies = [pltpu.make_async_copy(h_hbm.at[b], hid.at[b], sem.at[b]) for b in range(2)]
    for d, ref in enumerate((p0, p1, p2, p3)):
        pos = q ^ d
        half = pl.multiple_of((pos & 1) * (BLK * W), BLK * W)
        copies.append(pltpu.make_async_copy(
            ref, upper.at[pos >> 1, :, pl.ds(half, BLK * W)], sem.at[2 + d]))
    for copy in copies:
        copy.start()
    for copy in copies:
        copy.wait()
    for a in (-1, 0, 1):
        acc = None
        for b in range(2):
            term = lax.dot_general(
                upper[b], hid[b, :, (1 + a) * W:(9 + a) * W],
                (((1,), (1,)), ((), ())), preferred_element_type=F32)
            acc = term if acc is None else acc + term
        acc = (acc * scale).astype(BF16)
        for side in range(2):
            for owner, out in ((side, keep), (1 - side, give)):
                @pl.when(core == owner)
                def _(acc=acc, a=a, side=side, out=out):
                    for b in range(3):
                        for piece in range(8):
                            row = side * 128 + piece * 16
                            out[piece, 3 * (a + 1) + b] = acc[row:row + 16, b * C:b * C + C]


def wgrad(scale, ids, parts, hid):
    hbm = pl.BlockSpec(memory_space=pl.ANY)
    return pl.pallas_call(
        functools.partial(wgrad_kernel, scale),
        out_shape=(jax.ShapeDtypeStruct((8, 9, 16, C), BF16),) * 2,
        in_specs=[pl.BlockSpec(memory_space=pltpu.SMEM)] + [hbm] * 5,
        out_specs=(pl.BlockSpec(memory_space=pltpu.VMEM),) * 2,
        scratch_shapes=[
            pltpu.VMEM((2, C, 8 * W), BF16),
            pltpu.VMEM((2, 3 * C, 10 * W), BF16),
            pltpu.SemaphoreType.DMA((6,)),
        ],
        compiler_params=pltpu.CompilerParams(vmem_limit_bytes=40 << 20),
        cost_estimate=pl.CostEstimate(
            flops=2 * 9 * C * C * 2048, bytes_accessed=6 << 20, transcendentals=0),
        name="wgrad",
    )(ids, *parts, hid)


def place_kernel(ids, g0, g1, g2, g3, out):
    q = ids[0]
    for d, ref in enumerate((g0, g1, g2, g3)):
        pos = q ^ d
        half = pl.multiple_of((pos & 1) * (BLK * W), BLK * W)
        out[pos >> 1, :, pl.ds(half, BLK * W)] = ref[...]


def place(ids, parts):
    vm = pl.BlockSpec(memory_space=pltpu.VMEM)
    return pl.pallas_call(
        place_kernel,
        out_shape=jax.ShapeDtypeStruct((2, C, 8 * W), BF16),
        in_specs=[pl.BlockSpec(memory_space=pltpu.SMEM)] + [vm] * 4,
        out_specs=vm,
        cost_estimate=pl.CostEstimate(flops=0, bytes_accessed=2 << 20, transcendentals=0),
        name="place",
    )(ids, *parts)


def unpack_kernel(ids, near, far, out):
    core = ids[1]
    for chip in range(8):
        for side, ref in ((core, near), (1 - core, far)):
            row = pl.multiple_of(side * 128 + chip * 16, 16)
            out[:, pl.ds(row, 16), :] = ref[chip].astype(F32)


def unpack(ids, near, far):
    vm = pl.BlockSpec(memory_space=pltpu.VMEM)
    return pl.pallas_call(
        unpack_kernel,
        out_shape=jax.ShapeDtypeStruct((9, C, C), F32),
        in_specs=[pl.BlockSpec(memory_space=pltpu.SMEM)] + [vm] * 2,
        out_specs=vm,
        cost_estimate=pl.CostEstimate(flops=0, bytes_accessed=4 << 20, transcendentals=0),
        name="unpack",
    )(ids, near, far)


def per_device(acts, weights, cotangent):
    section = lax.axis_index(SECTION)
    tile = lax.axis_index(TILE)
    q = section & 3
    group = section >> 2
    core = tile & 1
    ids = jnp.stack([q, core]).astype(jnp.int32)
    n = BLK * W

    cot = lax.dynamic_slice(
        cotangent, (q >> 1, 0, (q & 1) * BLK, 0), (1, C, BLK, W)).reshape(C, n)

    wt = weights[0].transpose(2, 0, 1).reshape(C, 9 * C)
    w_half = lax.dynamic_slice(wt, (core * 128, 0), (128, 9 * C))
    flat = acts[0].reshape(2, C, 8 * W)

    def piece_of(member):
        return lax.dynamic_slice(flat, (member >> 1, 0, (member & 1) * n), (1, C, n))[0]

    pieces = [piece_of(q ^ d) for d in range(4)]
    w_half, pieces, cot = lax.optimization_barrier((w_half, pieces, cot))
    near_y = swap_member(w_half, 1)
    near_z = swap_member(w_half, 2)
    pieces = [pieces[0]] + [swap_member(pieces[d], d) for d in (1, 2, 3)]
    near_d = swap_member(near_y, 2)
    near = [near_y, near_z, near_d]
    slots = [wt] + near + [swap_core(block) for block in near]
    a_own, top, bottom = pack(ids, pieces)
    stored = (a_own, from_above(bottom), from_below(top))

    own = last = cot
    for tick in range(4):
        if tick:
            got = send(last, lambda s, t: (s - 4, t) if s >> 2 == 4 - tick else None)
            own = jnp.where(group == 3 - tick, got, own)
        if tick == 1:
            low = send(flat[:, :, 7 * W:], lambda s, t: (s, (t + 1) % 16))
            high = send(flat[:, :, :W], lambda s, t: (s, (t - 1) % 16))
            hid = hidden_shifts(jnp.concatenate([low, flat, high], axis=2))
        if tick == 3:
            own, hid = lax.optimization_barrier((own, hid))
        out_p, out_g, last = chain(ids, from_above(own), own, from_below(own), slots, stored)

    parts = [out_p[0]] + [swap_member(out_p[d], d) for d in (1, 2, 3)]
    grads = [out_g[0]] + [swap_member(out_g[d], d) for d in (1, 2, 3)]

    scale = 1.0 / (2 * 128 * 128) ** 0.5
    keep, give = wgrad(scale, ids, parts, hid)
    both = (keep.astype(F32) + swap_core(give).astype(F32)).astype(BF16)
    pieces = lax.all_to_all(both, ("x", "yhi"), 0, 0, tiled=True)
    total = jnp.sum(pieces.astype(F32), axis=0).astype(BF16)
    total, grads = lax.optimization_barrier((total, grads))
    copies = jnp.broadcast_to(total[None], (8,) + total.shape)
    gathered = lax.all_to_all(copies, ("x", "yhi"), 0, 0, tiled=True)
    weight_grad = unpack(ids, gathered, swap_core(gathered))

    grad_acts = place(ids, grads).reshape(1, 2, C, 8, W)
    return (grad_acts, weight_grad[None])


def solution(mesh):
    fine = Mesh(mesh.devices.reshape(16, 4, 2, 2), ("section", "x", "yhi", "core"))
    placed = (
        P(SECTION, None, None, TILE, None),
        P(SECTION, None, None, None),
        P(None, None, TILE, None),
    )
    return jax.shard_map(
        per_device,
        mesh=fine,
        in_specs=placed,
        out_specs=(P(SECTION, None, None, TILE, None), P(SECTION, None, None, None)),
        check_vma=False,
    )
```

```python
import functools

import jax
import jax.numpy as jnp
from jax import lax
from jax.experimental import pallas as pl
from jax.experimental.pallas import tpu as pltpu
from jax.sharding import Mesh, PartitionSpec as P

SECTION = "section"
TILE = ("x", "yhi", "core")
BOTH = (SECTION,) + TILE
C = 256
W = 128
LIMIT = 16 << 20
BLK = 4
F32 = jnp.float32
BF16 = jnp.bfloat16


def route(target):
    pairs = []
    for s in range(16):
        for t in range(16):
            to = target(s, t)
            if to is not None:
                pairs.append((s * 16 + t, to[0] * 16 + to[1]))
    return pairs


def send(block, target):
    return lax.ppermute(block, BOTH, route(target))


def swap_member(block, d):
    return send(block, lambda s, t: (s ^ d, t))


def swap_core(block):
    return send(block, lambda s, t: (s, t ^ 1))


def from_above(block):
    return send(block, lambda s, t: (s ^ 1, t if s & 1 == 0 else (t + 1) % 16))


def from_below(block):
    return send(block, lambda s, t: (s ^ 1, t if s & 1 == 1 else (t - 1) % 16))


def col_masks(rows):
    lane = lax.broadcasted_iota(jnp.int32, (rows, W), 1)
    return lane == 0, lane == W - 1


def col_shifts(x, first, last):
    before = jnp.where(first, 0.0, pltpu.roll(x, 1, 1))
    after = jnp.where(last, 0.0, pltpu.roll(x, W - 1, 1))
    return before, after


def pack_kernel(ids, p0, p1, p2, p3, own, top, bottom):
    q = ids[0]
    at = {3: 0, 2: 3, 1: 5}
    for layer in range(4):
        for d, ref in enumerate((p0, p1, p2, p3)):
            @pl.when((q ^ d) == layer)
            def _(layer=layer, ref=ref):
                own[layer] = ref[...]
                if layer:
                    lanes = slice(at[layer] * W, (at[layer] + layer) * W)
                    top[:, lanes] = ref[:, :layer * W]
                    bottom[:, lanes] = ref[:, (BLK - layer) * W:]


def pack(ids, pieces):
    vm = pl.BlockSpec(memory_space=pltpu.VMEM)
    return pl.pallas_call(
        pack_kernel,
        out_shape=(
            jax.ShapeDtypeStruct((4, C, BLK * W), BF16),
            jax.ShapeDtypeStruct((C, 6 * W), BF16),
            jax.ShapeDtypeStruct((C, 6 * W), BF16),
        ),
        in_specs=[pl.BlockSpec(memory_space=pltpu.SMEM)] + [vm] * 4,
        out_specs=(vm, vm, vm),
        cost_estimate=pl.CostEstimate(flops=0, bytes_accessed=3 << 20, transcendentals=0),
        compiler_params=pltpu.CompilerParams(vmem_limit_bytes=4 << 20),
        name="pack",
    )(ids, *pieces)


def gather_kernel(ids, w0, r1, r2, r3, c1, c2, c3, out, sem):
    core = ids[1]
    mine = pl.multiple_of(core * 128, 128)
    other = pl.multiple_of((1 - core) * 128, 128)
    copies = [pltpu.make_async_copy(w0, out.at[0], sem.at[0])]
    for d, (near, far) in enumerate(((r1, c1), (r2, c2), (r3, c3)), 1):
        copies += [
            pltpu.make_async_copy(near, out.at[d, pl.ds(mine, 128)], sem.at[d]),
            pltpu.make_async_copy(far, out.at[d, pl.ds(other, 128)], sem.at[3 + d]),
        ]
    for copy in copies:
        copy.start()
    for copy in copies:
        copy.wait()


def gather(ids, *blocks):
    return pl.pallas_call(
        gather_kernel,
        out_shape=jax.ShapeDtypeStruct((4, C, 9 * C), BF16),
        in_specs=[pl.BlockSpec(memory_space=pltpu.SMEM)]
        + [pl.BlockSpec(memory_space=pl.ANY)] * 7,
        out_specs=pl.BlockSpec(memory_space=pltpu.VMEM),
        scratch_shapes=[pltpu.SemaphoreType.DMA((7,))],
        compiler_params=pltpu.CompilerParams(vmem_limit_bytes=4 << 20),
        cost_estimate=pl.CostEstimate(flops=0, bytes_accessed=9 << 20, transcendentals=0),
        name="gather",
    )(ids, *blocks)


def chain_kernel(ids, up, own, dn, wbuf, vown, vup, vdn,
                 out_p, out_g, out_last, cat0, cat1):
    q = ids[0]
    first, last = col_masks(C)

    def put(cat, row, x32):
        before, after = col_shifts(x32, first, last)
        lanes = slice(row * W, row * W + W)
        cat[0:C, lanes] = after.astype(BF16)
        cat[C:2 * C, lanes] = x32.astype(BF16)
        cat[2 * C:3 * C, lanes] = before.astype(BF16)

    for part, ref in enumerate((up, own, dn)):
        for r in range(BLK):
            put(cat0, part * BLK + r, ref[:, r * W:r * W + W].astype(F32))

    at = {3: 0, 2: 3, 1: 5}

    def stored_row(layer, r):
        if r < layer:
            ref, row = vup, at[layer] + r
        elif r < layer + BLK:
            return vown[layer, :, (r - layer) * W:(r - layer + 1) * W].astype(F32)
        else:
            ref, row = vdn, at[layer] + r - layer - BLK
        return ref[:, row * W:row * W + W].astype(F32)

    cats = (cat0, cat1)
    for j in range(4):
        layer = 3 - j
        slot = q ^ layer
        cur, nxt = cats[j % 2], cats[(j + 1) % 2]
        rows_out = 10 - 2 * j
        out_p[slot] = cur[C:2 * C, (4 - j) * W:(8 - j) * W]
        for ch in range(rows_out // 2):
            back = None
            for a in (-1, 0, 1):
                start = (1 - a + 2 * ch) * W
                term = jnp.dot(
                    wbuf[slot, :, 768 * (a + 1):768 * (a + 2)],
                    cur[:, start:start + 2 * W],
                    preferred_element_type=F32,
                )
                back = term if back is None else back + term
            for r in (2 * ch, 2 * ch + 1):
                v = stored_row(layer, r)
                sig = 0.5 + 0.5 * jnp.tanh(0.5 * v)
                slope = sig * (1.0 + v * (1.0 - sig))
                mid = cur[C:2 * C, (1 + r) * W:(2 + r) * W].astype(F32)
                new = mid + back[:, (r - 2 * ch) * W:(r - 2 * ch + 1) * W] * slope
                if j < 3:
                    put(nxt, r, new)
                else:
                    out_last[:, r * W:r * W + W] = new.astype(BF16)
        if j < 3:
            out_g[slot] = nxt[C:2 * C, (3 - j) * W:(7 - j) * W]
        else:
            out_g[slot] = out_last[...]


def chain(ids, up, own, dn, weights, stored):
    vm = pl.BlockSpec(memory_space=pltpu.VMEM)
    n = BLK * W
    return pl.pallas_call(
        chain_kernel,
        out_shape=(
            jax.ShapeDtypeStruct((4, C, n), BF16),
            jax.ShapeDtypeStruct((4, C, n), BF16),
            jax.ShapeDtypeStruct((C, n), BF16),
        ),
        in_specs=[pl.BlockSpec(memory_space=pltpu.SMEM)] + [vm] * 7,
        out_specs=(vm, vm, vm),
        scratch_shapes=[
            pltpu.VMEM((3 * C, 12 * W), BF16),
            pltpu.VMEM((3 * C, 12 * W), BF16),
        ],
        compiler_params=pltpu.CompilerParams(vmem_limit_bytes=LIMIT),
        cost_estimate=pl.CostEstimate(
            flops=2 * 9 * C * C * 28 * W, bytes_accessed=10 << 20, transcendentals=28 * W * C),
        name="chain",
    )(ids, up, own, dn, weights, *stored)


def pick_kernel(turn, ids, got, own, out):
    out[...] = jnp.where(ids[2] == turn, got[...], own[...])


def pick(turn, ids, got, own):
    vm = pl.BlockSpec(memory_space=pltpu.VMEM)
    return pl.pallas_call(
        functools.partial(pick_kernel, turn),
        out_shape=jax.ShapeDtypeStruct(own.shape, own.dtype),
        in_specs=[pl.BlockSpec(memory_space=pltpu.SMEM), vm, vm],
        out_specs=vm,
        compiler_params=pltpu.CompilerParams(vmem_limit_bytes=4 << 20),
        cost_estimate=pl.CostEstimate(flops=0, bytes_accessed=1 << 19, transcendentals=0),
        name="pick",
    )(ids, got, own)


def hidden_kernel(low, flat, high, h_ref):
    first, last = col_masks(C)

    def put(lanes, v):
        v = v.astype(F32)
        hid = v * (0.5 + 0.5 * jnp.tanh(0.5 * v))
        before, after = col_shifts(hid, first, last)
        h_ref[0, 0:C, lanes] = before.astype(BF16)
        h_ref[0, C:2 * C, lanes] = hid.astype(BF16)
        h_ref[0, 2 * C:3 * C, lanes] = after.astype(BF16)

    put(slice(0, W), low[0])
    put(slice(9 * W, 10 * W), high[0])

    @pl.loop(0, 8)
    def _(r):
        put(pl.ds(pl.multiple_of(r * W + W, W), W),
            flat[0, :, pl.ds(pl.multiple_of(r * W, W), W)])


def hidden_shifts(low, flat, high):
    spec = lambda n: pl.BlockSpec((1, C, n), lambda b: (b, 0, 0))
    return pl.pallas_call(
        hidden_kernel,
        grid=(2,),
        out_shape=jax.ShapeDtypeStruct((2, 3 * C, 10 * W), BF16),
        in_specs=[spec(W), spec(8 * W), spec(W)],
        out_specs=pl.BlockSpec((1, 3 * C, 10 * W), lambda b: (b, 0, 0)),
        compiler_params=pltpu.CompilerParams(vmem_limit_bytes=LIMIT),
        cost_estimate=pl.CostEstimate(
            flops=10 * 2 * C * 10 * W, bytes_accessed=6 << 20, transcendentals=2 * C * 10 * W),
        name="hidden",
    )(low, flat, high)


def wgrad_kernel(scale, ids, p0, p1, p2, p3, h_hbm, keep, give, upper, hid, sem):
    q = ids[0]
    core = ids[1]
    copies = [pltpu.make_async_copy(h_hbm.at[b], hid.at[b], sem.at[b]) for b in range(2)]
    for d, ref in enumerate((p0, p1, p2, p3)):
        pos = q ^ d
        half = pl.multiple_of((pos & 1) * (BLK * W), BLK * W)
        copies.append(pltpu.make_async_copy(
            ref, upper.at[pos >> 1, :, pl.ds(half, BLK * W)], sem.at[2 + d]))
    for copy in copies:
        copy.start()
    for copy in copies:
        copy.wait()
    @pl.loop(0, 3)
    def _(step):
        acc = None
        for b in range(2):
            term = lax.dot_general(
                upper[b], hid[b, :, pl.ds(pl.multiple_of(step * W, W), 8 * W)],
                (((1,), (1,)), ((), ())), preferred_element_type=F32)
            acc = term if acc is None else acc + term
        acc = (acc * scale).astype(BF16)
        for side in range(2):
            for owner, out in ((side, keep), (1 - side, give)):
                @pl.when(core == owner)
                def _(acc=acc, side=side, out=out):
                    for b in range(3):
                        for piece in range(8):
                            row = side * 128 + piece * 16
                            out[piece, 3 * step + b] = acc[row:row + 16, b * C:b * C + C]


def wgrad(scale, ids, parts, hid):
    hbm = pl.BlockSpec(memory_space=pl.ANY)
    return pl.pallas_call(
        functools.partial(wgrad_kernel, scale),
        out_shape=(jax.ShapeDtypeStruct((8, 9, 16, C), BF16),) * 2,
        in_specs=[pl.BlockSpec(memory_space=pltpu.SMEM)] + [hbm] * 5,
        out_specs=(pl.BlockSpec(memory_space=pltpu.VMEM),) * 2,
        scratch_shapes=[
            pltpu.VMEM((2, C, 8 * W), BF16),
            pltpu.VMEM((2, 3 * C, 10 * W), BF16),
            pltpu.SemaphoreType.DMA((6,)),
        ],
        compiler_params=pltpu.CompilerParams(vmem_limit_bytes=LIMIT),
        cost_estimate=pl.CostEstimate(
            flops=2 * 9 * C * C * 2048, bytes_accessed=6 << 20, transcendentals=0),
        name="wgrad",
    )(ids, *parts, hid)


def place_kernel(ids, g0, g1, g2, g3, out):
    q = ids[0]
    for d, ref in enumerate((g0, g1, g2, g3)):
        pos = q ^ d
        half = pl.multiple_of((pos & 1) * (BLK * W), BLK * W)
        out[pos >> 1, :, pl.ds(half, BLK * W)] = ref[...]


def place(ids, parts):
    vm = pl.BlockSpec(memory_space=pltpu.VMEM)
    return pl.pallas_call(
        place_kernel,
        out_shape=jax.ShapeDtypeStruct((2, C, 8 * W), BF16),
        in_specs=[pl.BlockSpec(memory_space=pltpu.SMEM)] + [vm] * 4,
        out_specs=vm,
        cost_estimate=pl.CostEstimate(flops=0, bytes_accessed=2 << 20, transcendentals=0),
        compiler_params=pltpu.CompilerParams(vmem_limit_bytes=4 << 20),
        name="place",
    )(ids, *parts)


def unpack_kernel(ids, near, far, out):
    core = ids[1]
    for chip in range(8):
        for side, ref in ((core, near), (1 - core, far)):
            row = pl.multiple_of(side * 128 + chip * 16, 16)
            out[:, pl.ds(row, 16), :] = ref[chip].astype(F32)


def unpack(ids, near, far):
    vm = pl.BlockSpec(memory_space=pltpu.VMEM)
    return pl.pallas_call(
        unpack_kernel,
        out_shape=jax.ShapeDtypeStruct((9, C, C), F32),
        in_specs=[pl.BlockSpec(memory_space=pltpu.SMEM)] + [vm] * 2,
        out_specs=vm,
        cost_estimate=pl.CostEstimate(flops=0, bytes_accessed=4 << 20, transcendentals=0),
        compiler_params=pltpu.CompilerParams(vmem_limit_bytes=4 << 20),
        name="unpack",
    )(ids, near, far)


def per_device(acts, weights, cotangent):
    section = lax.axis_index(SECTION)
    tile = lax.axis_index(TILE)
    q = section & 3
    group = section >> 2
    core = tile & 1
    ids = jnp.stack([q, core, group]).astype(jnp.int32)
    n = BLK * W

    cot = lax.dynamic_slice(
        cotangent, (q >> 1, 0, (q & 1) * BLK, 0), (1, C, BLK, W)).reshape(C, n)

    wt = weights[0].transpose(2, 0, 1).reshape(C, 9 * C)
    w_half = lax.dynamic_slice(wt, (core * 128, 0), (128, 9 * C))
    flat = acts[0].reshape(2, C, 8 * W)

    def piece_of(member):
        return lax.dynamic_slice(flat, (member >> 1, 0, (member & 1) * n), (1, C, n))[0]

    pieces = [piece_of(q ^ d) for d in range(4)]
    rims = (flat[:, :, 7 * W:], flat[:, :, :W])
    w_half, pieces, cot, rims = lax.optimization_barrier((w_half, pieces, cot, rims))
    near_y = swap_member(w_half, 1)
    near_z = swap_member(w_half, 2)
    pieces = [pieces[0]] + [swap_member(pieces[d], d) for d in (1, 2, 3)]
    near_y, near_z, pieces, cot = lax.optimization_barrier((near_y, near_z, pieces, cot))
    up, dn = from_above(cot), from_below(cot)
    a_own, top, bottom = pack(ids, pieces)
    stored = (a_own, from_above(bottom), from_below(top))
    near_d = swap_member(near_y, 2)
    near = (near_y, near_z, near_d)
    slots = gather(ids, wt, *near, *[swap_core(block) for block in near])

    own = last = cot
    for tick in range(4):
        if tick:
            got = send(last, lambda s, t: (s - 4, t) if s >> 2 == 4 - tick else None)
            own = pick(3 - tick, ids, got, own)
            up, dn = from_above(own), from_below(own)
        if tick == 1:
            low = send(rims[0], lambda s, t: (s, (t + 1) % 16))
            high = send(rims[1], lambda s, t: (s, (t - 1) % 16))
            hid = hidden_shifts(low, flat, high)
        if tick == 2:
            up, hid = lax.optimization_barrier((up, hid))
        out_p, out_g, last = chain(ids, up, own, dn, slots, stored)

    parts = [out_p[0]] + [swap_member(out_p[d], d) for d in (1, 2, 3)]
    grads = [out_g[0]] + [swap_member(out_g[d], d) for d in (1, 2, 3)]

    scale = 1.0 / (2 * 128 * 128) ** 0.5
    keep, give = wgrad(scale, ids, parts, hid)
    both = (keep.astype(F32) + swap_core(give).astype(F32)).astype(BF16)
    pieces = lax.all_to_all(both, ("x", "yhi"), 0, 0, tiled=True)
    total = jnp.sum(pieces.astype(F32), axis=0).astype(BF16)
    total, grads = lax.optimization_barrier((total, grads))
    copies = jnp.broadcast_to(total[None], (8,) + total.shape)
    gathered = lax.all_to_all(copies, ("x", "yhi"), 0, 0, tiled=True)
    weight_grad = unpack(ids, gathered, swap_core(gathered))

    grad_acts = place(ids, grads).reshape(1, 2, C, 8, W)
    return (grad_acts, weight_grad[None])


def solution(mesh):
    fine = Mesh(mesh.devices.reshape(16, 4, 2, 2), ("section", "x", "yhi", "core"))
    placed = (
        P(SECTION, None, None, TILE, None),
        P(SECTION, None, None, None),
        P(None, None, TILE, None),
    )
    return jax.shard_map(
        per_device,
        mesh=fine,
        in_specs=placed,
        out_specs=(P(SECTION, None, None, TILE, None), P(SECTION, None, None, None)),
        check_vma=False,
    )
```

```python
import functools

import jax
import jax.numpy as jnp
from jax import lax
from jax.experimental import pallas as pl
from jax.experimental.pallas import tpu as pltpu
from jax.sharding import Mesh, PartitionSpec as P

SECTION = "section"
TILE = ("x", "yhi", "core")
BOTH = (SECTION,) + TILE
C = 256
W = 128
LIMIT = 16 << 20
BLK = 4
F32 = jnp.float32
BF16 = jnp.bfloat16


def route(target):
    pairs = []
    for s in range(16):
        for t in range(16):
            to = target(s, t)
            if to is not None:
                pairs.append((s * 16 + t, to[0] * 16 + to[1]))
    return pairs


def send(block, target):
    return lax.ppermute(block, BOTH, route(target))


def swap_member(block, d):
    return send(block, lambda s, t: (s ^ d, t))


def swap_core(block):
    return send(block, lambda s, t: (s, t ^ 1))


def from_above(block):
    return send(block, lambda s, t: (s ^ 1, t if s & 1 == 0 else (t + 1) % 16))


def from_below(block):
    return send(block, lambda s, t: (s ^ 1, t if s & 1 == 1 else (t - 1) % 16))


def col_masks(rows):
    lane = lax.broadcasted_iota(jnp.int32, (rows, W), 1)
    return lane == 0, lane == W - 1


def col_shifts(x, first, last):
    before = jnp.where(first, 0.0, pltpu.roll(x, 1, 1))
    after = jnp.where(last, 0.0, pltpu.roll(x, W - 1, 1))
    return before, after


def pack_kernel(ids, p0, p1, p2, p3, own, top, bottom):
    q = ids[0]
    at = {3: 0, 2: 3, 1: 5}
    for layer in range(4):
        for d, ref in enumerate((p0, p1, p2, p3)):
            @pl.when((q ^ d) == layer)
            def _(layer=layer, ref=ref):
                own[layer] = ref[...]
                if layer:
                    lanes = slice(at[layer] * W, (at[layer] + layer) * W)
                    top[:, lanes] = ref[:, :layer * W]
                    bottom[:, lanes] = ref[:, (BLK - layer) * W:]


def pack(ids, pieces):
    vm = pl.BlockSpec(memory_space=pltpu.VMEM)
    return pl.pallas_call(
        pack_kernel,
        out_shape=(
            jax.ShapeDtypeStruct((4, C, BLK * W), BF16),
            jax.ShapeDtypeStruct((C, 6 * W), BF16),
            jax.ShapeDtypeStruct((C, 6 * W), BF16),
        ),
        in_specs=[pl.BlockSpec(memory_space=pltpu.SMEM)] + [vm] * 4,
        out_specs=(vm, vm, vm),
        cost_estimate=pl.CostEstimate(flops=0, bytes_accessed=3 << 20, transcendentals=0),
        compiler_params=pltpu.CompilerParams(vmem_limit_bytes=4 << 20),
        name="pack",
    )(ids, *pieces)


def gather_kernel(ids, w0, r1, r2, r3, c1, c2, c3, out, sem):
    core = ids[1]
    mine = pl.multiple_of(core * 128, 128)
    other = pl.multiple_of((1 - core) * 128, 128)
    copies = [pltpu.make_async_copy(w0, out.at[0], sem.at[0])]
    for d, (near, far) in enumerate(((r1, c1), (r2, c2), (r3, c3)), 1):
        copies += [
            pltpu.make_async_copy(near, out.at[d, pl.ds(mine, 128)], sem.at[d]),
            pltpu.make_async_copy(far, out.at[d, pl.ds(other, 128)], sem.at[3 + d]),
        ]
    for copy in copies:
        copy.start()
    for copy in copies:
        copy.wait()


def gather(ids, *blocks):
    return pl.pallas_call(
        gather_kernel,
        out_shape=jax.ShapeDtypeStruct((4, C, 9 * C), BF16),
        in_specs=[pl.BlockSpec(memory_space=pltpu.SMEM)]
        + [pl.BlockSpec(memory_space=pl.ANY)] * 7,
        out_specs=pl.BlockSpec(memory_space=pltpu.VMEM),
        scratch_shapes=[pltpu.SemaphoreType.DMA((7,))],
        compiler_params=pltpu.CompilerParams(vmem_limit_bytes=4 << 20),
        cost_estimate=pl.CostEstimate(flops=0, bytes_accessed=9 << 20, transcendentals=0),
        name="gather",
    )(ids, *blocks)


def chain_kernel(final, ids, up, own, dn, wbuf, vown, vup, vdn, *refs):
    q = ids[0]
    cat0, cat1 = refs[-2:]
    if final:
        out_p, out_g = refs[:2]
    else:
        out_last = refs[0]
    first, last = col_masks(C)

    def put(cat, row, x32):
        before, after = col_shifts(x32, first, last)
        lanes = slice(row * W, row * W + W)
        cat[0:C, lanes] = after.astype(BF16)
        cat[C:2 * C, lanes] = x32.astype(BF16)
        cat[2 * C:3 * C, lanes] = before.astype(BF16)

    for part, ref in enumerate((up, own, dn)):
        for r in range(BLK):
            put(cat0, part * BLK + r, ref[:, r * W:r * W + W].astype(F32))

    at = {3: 0, 2: 3, 1: 5}

    def stored_row(layer, r):
        if r < layer:
            ref, row = vup, at[layer] + r
        elif r < layer + BLK:
            return vown[layer, :, (r - layer) * W:(r - layer + 1) * W].astype(F32)
        else:
            ref, row = vdn, at[layer] + r - layer - BLK
        return ref[:, row * W:row * W + W].astype(F32)

    cats = (cat0, cat1)
    for j in range(4):
        layer = 3 - j
        slot = q ^ layer
        cur, nxt = cats[j % 2], cats[(j + 1) % 2]
        rows_out = 10 - 2 * j
        if final:
            out_p[slot] = cur[C:2 * C, (4 - j) * W:(8 - j) * W]
        for ch in range(rows_out // 2):
            back = None
            for a in (-1, 0, 1):
                start = (1 - a + 2 * ch) * W
                term = jnp.dot(
                    wbuf[slot, :, 768 * (a + 1):768 * (a + 2)],
                    cur[:, start:start + 2 * W],
                    preferred_element_type=F32,
                )
                back = term if back is None else back + term
            for r in (2 * ch, 2 * ch + 1):
                v = stored_row(layer, r)
                sig = 0.5 + 0.5 * jnp.tanh(0.5 * v)
                slope = sig * (1.0 + v * (1.0 - sig))
                mid = cur[C:2 * C, (1 + r) * W:(2 + r) * W].astype(F32)
                new = mid + back[:, (r - 2 * ch) * W:(r - 2 * ch + 1) * W] * slope
                if j < 3:
                    put(nxt, r, new)
                elif final:
                    out_g[slot, :, r * W:r * W + W] = new.astype(BF16)
                else:
                    out_last[:, r * W:r * W + W] = new.astype(BF16)
        if final and j < 3:
            out_g[slot] = nxt[C:2 * C, (3 - j) * W:(7 - j) * W]


def chain(final, ids, up, own, dn, weights, stored):
    vm = pl.BlockSpec(memory_space=pltpu.VMEM)
    n = BLK * W
    if final:
        out_shape = (jax.ShapeDtypeStruct((4, C, n), BF16),) * 2
    else:
        out_shape = jax.ShapeDtypeStruct((C, n), BF16)
    return pl.pallas_call(
        functools.partial(chain_kernel, final),
        out_shape=out_shape,
        in_specs=[pl.BlockSpec(memory_space=pltpu.SMEM)] + [vm] * 7,
        out_specs=(vm, vm) if final else vm,
        scratch_shapes=[
            pltpu.VMEM((3 * C, 12 * W), BF16),
            pltpu.VMEM((3 * C, 12 * W), BF16),
        ],
        compiler_params=pltpu.CompilerParams(vmem_limit_bytes=LIMIT),
        cost_estimate=pl.CostEstimate(
            flops=2 * 9 * C * C * 28 * W, bytes_accessed=10 << 20, transcendentals=28 * W * C),
        name="chain",
    )(ids, up, own, dn, weights, *stored)


def pick_kernel(turn, ids, got, own, out):
    out[...] = jnp.where(ids[2] == turn, got[...], own[...])


def pick(turn, ids, got, own):
    vm = pl.BlockSpec(memory_space=pltpu.VMEM)
    return pl.pallas_call(
        functools.partial(pick_kernel, turn),
        out_shape=jax.ShapeDtypeStruct(own.shape, own.dtype),
        in_specs=[pl.BlockSpec(memory_space=pltpu.SMEM), vm, vm],
        out_specs=vm,
        compiler_params=pltpu.CompilerParams(vmem_limit_bytes=4 << 20),
        cost_estimate=pl.CostEstimate(flops=0, bytes_accessed=1 << 19, transcendentals=0),
        name="pick",
    )(ids, got, own)


def hidden_kernel(low, flat, high, h_ref):
    first, last = col_masks(C)

    def put(lanes, v):
        v = v.astype(F32)
        hid = v * (0.5 + 0.5 * jnp.tanh(0.5 * v))
        before, after = col_shifts(hid, first, last)
        h_ref[0, 0:C, lanes] = before.astype(BF16)
        h_ref[0, C:2 * C, lanes] = hid.astype(BF16)
        h_ref[0, 2 * C:3 * C, lanes] = after.astype(BF16)

    put(slice(0, W), low[0])
    put(slice(9 * W, 10 * W), high[0])

    @pl.loop(0, 8)
    def _(r):
        put(pl.ds(pl.multiple_of(r * W + W, W), W),
            flat[0, :, pl.ds(pl.multiple_of(r * W, W), W)])


def hidden_shifts(low, flat, high):
    spec = lambda n: pl.BlockSpec((1, C, n), lambda b: (b, 0, 0))
    return pl.pallas_call(
        hidden_kernel,
        grid=(2,),
        out_shape=jax.ShapeDtypeStruct((2, 3 * C, 10 * W), BF16),
        in_specs=[spec(W), spec(8 * W), spec(W)],
        out_specs=pl.BlockSpec((1, 3 * C, 10 * W), lambda b: (b, 0, 0)),
        compiler_params=pltpu.CompilerParams(vmem_limit_bytes=LIMIT),
        cost_estimate=pl.CostEstimate(
            flops=10 * 2 * C * 10 * W, bytes_accessed=6 << 20, transcendentals=2 * C * 10 * W),
        name="hidden",
    )(low, flat, high)


def wgrad_kernel(scale, ids, p0, p1, p2, p3, h_hbm, keep, give, upper, hid, sem):
    q = ids[0]
    core = ids[1]
    copies = [pltpu.make_async_copy(h_hbm.at[b], hid.at[b], sem.at[b]) for b in range(2)]
    for d, ref in enumerate((p0, p1, p2, p3)):
        pos = q ^ d
        half = pl.multiple_of((pos & 1) * (BLK * W), BLK * W)
        copies.append(pltpu.make_async_copy(
            ref, upper.at[pos >> 1, :, pl.ds(half, BLK * W)], sem.at[2 + d]))
    for copy in copies:
        copy.start()
    for copy in copies:
        copy.wait()
    @pl.loop(0, 3)
    def _(step):
        acc = None
        for b in range(2):
            term = lax.dot_general(
                upper[b], hid[b, :, pl.ds(pl.multiple_of(step * W, W), 8 * W)],
                (((1,), (1,)), ((), ())), preferred_element_type=F32)
            acc = term if acc is None else acc + term
        acc = (acc * scale).astype(BF16)
        for side in range(2):
            for owner, out in ((side, keep), (1 - side, give)):
                @pl.when(core == owner)
                def _(acc=acc, side=side, out=out):
                    for b in range(3):
                        for piece in range(8):
                            row = side * 128 + piece * 16
                            out[piece, 3 * step + b] = acc[row:row + 16, b * C:b * C + C]


def wgrad(scale, ids, parts, hid):
    hbm = pl.BlockSpec(memory_space=pl.ANY)
    return pl.pallas_call(
        functools.partial(wgrad_kernel, scale),
        out_shape=(jax.ShapeDtypeStruct((8, 9, 16, C), BF16),) * 2,
        in_specs=[pl.BlockSpec(memory_space=pltpu.SMEM)] + [hbm] * 5,
        out_specs=(pl.BlockSpec(memory_space=pltpu.VMEM),) * 2,
        scratch_shapes=[
            pltpu.VMEM((2, C, 8 * W), BF16),
            pltpu.VMEM((2, 3 * C, 10 * W), BF16),
            pltpu.SemaphoreType.DMA((6,)),
        ],
        compiler_params=pltpu.CompilerParams(vmem_limit_bytes=LIMIT),
        cost_estimate=pl.CostEstimate(
            flops=2 * 9 * C * C * 2048, bytes_accessed=6 << 20, transcendentals=0),
        name="wgrad",
    )(ids, *parts, hid)


def place_kernel(ids, g0, g1, g2, g3, out):
    q = ids[0]
    for d, ref in enumerate((g0, g1, g2, g3)):
        pos = q ^ d
        half = pl.multiple_of((pos & 1) * (BLK * W), BLK * W)
        out[pos >> 1, :, pl.ds(half, BLK * W)] = ref[...]


def place(ids, parts):
    vm = pl.BlockSpec(memory_space=pltpu.VMEM)
    return pl.pallas_call(
        place_kernel,
        out_shape=jax.ShapeDtypeStruct((2, C, 8 * W), BF16),
        in_specs=[pl.BlockSpec(memory_space=pltpu.SMEM)] + [vm] * 4,
        out_specs=vm,
        cost_estimate=pl.CostEstimate(flops=0, bytes_accessed=2 << 20, transcendentals=0),
        compiler_params=pltpu.CompilerParams(vmem_limit_bytes=4 << 20),
        name="place",
    )(ids, *parts)


def unpack_kernel(ids, near, far, out):
    core = ids[1]
    for chip in range(8):
        for side, ref in ((core, near), (1 - core, far)):
            row = pl.multiple_of(side * 128 + chip * 16, 16)
            out[:, pl.ds(row, 16), :] = ref[chip].astype(F32)


def unpack(ids, near, far):
    vm = pl.BlockSpec(memory_space=pltpu.VMEM)
    return pl.pallas_call(
        unpack_kernel,
        out_shape=jax.ShapeDtypeStruct((9, C, C), F32),
        in_specs=[pl.BlockSpec(memory_space=pltpu.SMEM)] + [vm] * 2,
        out_specs=vm,
        cost_estimate=pl.CostEstimate(flops=0, bytes_accessed=4 << 20, transcendentals=0),
        compiler_params=pltpu.CompilerParams(vmem_limit_bytes=4 << 20),
        name="unpack",
    )(ids, near, far)


def per_device(acts, weights, cotangent):
    section = lax.axis_index(SECTION)
    tile = lax.axis_index(TILE)
    q = section & 3
    group = section >> 2
    core = tile & 1
    ids = jnp.stack([q, core, group]).astype(jnp.int32)
    n = BLK * W

    cot = lax.dynamic_slice(
        cotangent.reshape(2, C, 8 * W), (q >> 1, 0, (q & 1) * n), (1, C, n))[0]

    wt = weights[0].transpose(2, 0, 1).reshape(C, 9 * C)
    w_half = lax.dynamic_slice(wt, (core * 128, 0), (128, 9 * C))
    flat = acts[0].reshape(2, C, 8 * W)

    def piece_of(member):
        return lax.dynamic_slice(flat, (member >> 1, 0, (member & 1) * n), (1, C, n))[0]

    pieces = [piece_of(q ^ d) for d in range(4)]
    rims = (flat[:, :, 7 * W:], flat[:, :, :W])
    w_half, pieces, cot, rims, ids = lax.optimization_barrier((w_half, pieces, cot, rims, ids))
    near_y = swap_member(w_half, 1)
    near_z = swap_member(w_half, 2)
    pieces = [pieces[0]] + [swap_member(pieces[d], d) for d in (1, 2, 3)]
    near_y, near_z, pieces = lax.optimization_barrier((near_y, near_z, pieces))
    near_d = swap_member(near_y, 2)
    a_own, top, bottom = pack(ids, pieces)
    vup, vdn = from_above(bottom), from_below(top)
    top, bottom, cot = lax.optimization_barrier((top, bottom, cot))
    up, dn = from_above(cot), from_below(cot)
    near_d, near_y, near_z, vup, vdn, up, dn = lax.optimization_barrier(
        (near_d, near_y, near_z, vup, vdn, up, dn))
    near = (near_y, near_z, near_d)
    slots = gather(ids, wt, *near, *[swap_core(block) for block in near])
    stored = (a_own, vup, vdn)

    own = last = cot
    for tick in range(4):
        if tick:
            got = send(last, lambda s, t: (s - 4, t) if s >> 2 == 4 - tick else None)
            own = pick(3 - tick, ids, got, own)
            up, dn = from_above(own), from_below(own)
        if tick == 1:
            low = send(rims[0], lambda s, t: (s, (t + 1) % 16))
            high = send(rims[1], lambda s, t: (s, (t - 1) % 16))
            hid = hidden_shifts(low, flat, high)
        if tick == 2:
            up, hid = lax.optimization_barrier((up, hid))
        last = chain(tick == 3, ids, up, own, dn, slots, stored)
    out_p, out_g = last

    parts = [out_p[0]] + [swap_member(out_p[d], d) for d in (1, 2, 3)]
    grads = [out_g[0]] + [swap_member(out_g[d], d) for d in (1, 2, 3)]

    scale = 1.0 / (2 * 128 * 128) ** 0.5
    keep, give = wgrad(scale, ids, parts, hid)
    both = (keep.astype(F32) + swap_core(give).astype(F32)).astype(BF16)
    both, grads = lax.optimization_barrier((both, grads))
    pieces = lax.all_to_all(both, ("x", "yhi"), 0, 0, tiled=True)
    total = jnp.sum(pieces.astype(F32), axis=0).astype(BF16)
    copies = jnp.broadcast_to(total[None], (8,) + total.shape)
    gathered = lax.all_to_all(copies, ("x", "yhi"), 0, 0, tiled=True)
    weight_grad = unpack(ids, gathered, swap_core(gathered))

    grad_acts = place(ids, grads).reshape(1, 2, C, 8, W)
    return (grad_acts, weight_grad[None])


def solution(mesh):
    fine = Mesh(mesh.devices.reshape(16, 4, 2, 2), ("section", "x", "yhi", "core"))
    placed = (
        P(SECTION, None, None, TILE, None),
        P(SECTION, None, None, None),
        P(None, None, TILE, None),
    )
    return jax.shard_map(
        per_device,
        mesh=fine,
        in_specs=placed,
        out_specs=(P(SECTION, None, None, TILE, None), P(SECTION, None, None, None)),
        check_vma=False,
    )
```

```python
import functools

import jax
import jax.numpy as jnp
from jax import lax
from jax.experimental import pallas as pl
from jax.experimental.pallas import tpu as pltpu
from jax.sharding import Mesh, PartitionSpec as P

SECTION = "section"
TILE = ("x", "yhi", "core")
BOTH = (SECTION,) + TILE
C = 256
W = 128
LIMIT = 16 << 20
BLK = 4
F32 = jnp.float32
BF16 = jnp.bfloat16


def route(target):
    pairs = []
    for s in range(16):
        for t in range(16):
            to = target(s, t)
            if to is not None:
                pairs.append((s * 16 + t, to[0] * 16 + to[1]))
    return pairs


def send(block, target):
    return lax.ppermute(block, BOTH, route(target))


def swap_member(block, d):
    return send(block, lambda s, t: (s ^ d, t))


def swap_core(block):
    return send(block, lambda s, t: (s, t ^ 1))


def from_above(block):
    return send(block, lambda s, t: (s ^ 1, t if s & 1 == 0 else (t + 1) % 16))


def from_below(block):
    return send(block, lambda s, t: (s ^ 1, t if s & 1 == 1 else (t - 1) % 16))


def col_masks(rows):
    lane = lax.broadcasted_iota(jnp.int32, (rows, W), 1)
    return lane == 0, lane == W - 1


def col_shifts(x, first, last):
    before = jnp.where(first, 0.0, pltpu.roll(x, 1, 1))
    after = jnp.where(last, 0.0, pltpu.roll(x, W - 1, 1))
    return before, after


def pack_kernel(ids, p0, p1, p2, p3, own, top, bottom):
    q = ids[0]
    at = {3: 0, 2: 3, 1: 5}
    for layer in range(4):
        for d, ref in enumerate((p0, p1, p2, p3)):
            @pl.when((q ^ d) == layer)
            def _(layer=layer, ref=ref):
                own[layer] = ref[...]
                if layer:
                    lanes = slice(at[layer] * W, (at[layer] + layer) * W)
                    top[:, lanes] = ref[:, :layer * W]
                    bottom[:, lanes] = ref[:, (BLK - layer) * W:]


def pack(ids, pieces):
    vm = pl.BlockSpec(memory_space=pltpu.VMEM)
    return pl.pallas_call(
        pack_kernel,
        out_shape=(
            jax.ShapeDtypeStruct((4, C, BLK * W), BF16),
            jax.ShapeDtypeStruct((C, 6 * W), BF16),
            jax.ShapeDtypeStruct((C, 6 * W), BF16),
        ),
        in_specs=[pl.BlockSpec(memory_space=pltpu.SMEM)] + [vm] * 4,
        out_specs=(vm, vm, vm),
        cost_estimate=pl.CostEstimate(flops=0, bytes_accessed=3 << 20, transcendentals=0),
        compiler_params=pltpu.CompilerParams(vmem_limit_bytes=4 << 20),
        name="pack",
    )(ids, *pieces)


def gather_kernel(ids, w0, r1, r2, r3, c1, c2, c3, out, sem):
    core = ids[1]
    mine = pl.multiple_of(core * 128, 128)
    other = pl.multiple_of((1 - core) * 128, 128)
    copies = [pltpu.make_async_copy(w0, out.at[0], sem.at[0])]
    for d, (near, far) in enumerate(((r1, c1), (r2, c2), (r3, c3)), 1):
        copies += [
            pltpu.make_async_copy(near, out.at[d, pl.ds(mine, 128)], sem.at[d]),
            pltpu.make_async_copy(far, out.at[d, pl.ds(other, 128)], sem.at[3 + d]),
        ]
    for copy in copies:
        copy.start()
    for copy in copies:
        copy.wait()


def gather(ids, *blocks):
    return pl.pallas_call(
        gather_kernel,
        out_shape=jax.ShapeDtypeStruct((4, C, 9 * C), BF16),
        in_specs=[pl.BlockSpec(memory_space=pltpu.SMEM)]
        + [pl.BlockSpec(memory_space=pl.ANY)] * 7,
        out_specs=pl.BlockSpec(memory_space=pltpu.VMEM),
        scratch_shapes=[pltpu.SemaphoreType.DMA((7,))],
        compiler_params=pltpu.CompilerParams(vmem_limit_bytes=4 << 20),
        cost_estimate=pl.CostEstimate(flops=0, bytes_accessed=9 << 20, transcendentals=0),
        name="gather",
    )(ids, *blocks)


def chain_kernel(final, ids, up, own, dn, wbuf, vown, vup, vdn, *refs):
    q = ids[0]
    cat0, cat1 = refs[-2:]
    if final:
        out_p, out_g = refs[:2]
    else:
        out_last = refs[0]
    first, last = col_masks(C)

    def put(cat, row, x32):
        before, after = col_shifts(x32, first, last)
        lanes = slice(row * W, row * W + W)
        cat[0:C, lanes] = after.astype(BF16)
        cat[C:2 * C, lanes] = x32.astype(BF16)
        cat[2 * C:3 * C, lanes] = before.astype(BF16)

    for part, ref in enumerate((up, own, dn)):
        for r in range(BLK):
            put(cat0, part * BLK + r, ref[:, r * W:r * W + W].astype(F32))

    at = {3: 0, 2: 3, 1: 5}

    def stored_row(layer, r):
        if r < layer:
            ref, row = vup, at[layer] + r
        elif r < layer + BLK:
            return vown[layer, :, (r - layer) * W:(r - layer + 1) * W].astype(F32)
        else:
            ref, row = vdn, at[layer] + r - layer - BLK
        return ref[:, row * W:row * W + W].astype(F32)

    cats = (cat0, cat1)
    for j in range(4):
        layer = 3 - j
        slot = q ^ layer
        cur, nxt = cats[j % 2], cats[(j + 1) % 2]
        rows_out = 10 - 2 * j
        if final:
            out_p[slot] = cur[C:2 * C, (4 - j) * W:(8 - j) * W]
        for ch in range(rows_out // 2):
            back = None
            for a in (-1, 0, 1):
                start = (1 - a + 2 * ch) * W
                term = jnp.dot(
                    wbuf[slot, :, 768 * (a + 1):768 * (a + 2)],
                    cur[:, start:start + 2 * W],
                    preferred_element_type=F32,
                )
                back = term if back is None else back + term
            for r in (2 * ch, 2 * ch + 1):
                v = stored_row(layer, r)
                sig = 0.5 + 0.5 * jnp.tanh(0.5 * v)
                slope = sig * (1.0 + v * (1.0 - sig))
                mid = cur[C:2 * C, (1 + r) * W:(2 + r) * W].astype(F32)
                new = mid + back[:, (r - 2 * ch) * W:(r - 2 * ch + 1) * W] * slope
                if j < 3:
                    put(nxt, r, new)
                elif final:
                    out_g[slot, :, r * W:r * W + W] = new.astype(BF16)
                else:
                    out_last[:, r * W:r * W + W] = new.astype(BF16)
        if final and j < 3:
            out_g[slot] = nxt[C:2 * C, (3 - j) * W:(7 - j) * W]


def chain(final, ids, up, own, dn, weights, stored):
    vm = pl.BlockSpec(memory_space=pltpu.VMEM)
    n = BLK * W
    if final:
        out_shape = (jax.ShapeDtypeStruct((4, C, n), BF16),) * 2
    else:
        out_shape = jax.ShapeDtypeStruct((C, n), BF16)
    return pl.pallas_call(
        functools.partial(chain_kernel, final),
        out_shape=out_shape,
        in_specs=[pl.BlockSpec(memory_space=pltpu.SMEM)] + [vm] * 7,
        out_specs=(vm, vm) if final else vm,
        scratch_shapes=[
            pltpu.VMEM((3 * C, 12 * W), BF16),
            pltpu.VMEM((3 * C, 12 * W), BF16),
        ],
        compiler_params=pltpu.CompilerParams(vmem_limit_bytes=LIMIT),
        cost_estimate=pl.CostEstimate(
            flops=2 * 9 * C * C * 28 * W, bytes_accessed=10 << 20, transcendentals=28 * W * C),
        name="chain",
    )(ids, up, own, dn, weights, *stored)


def pick_kernel(turn, ids, got, own, out):
    out[...] = jnp.where(ids[2] == turn, got[...], own[...])


def pick(turn, ids, got, own):
    vm = pl.BlockSpec(memory_space=pltpu.VMEM)
    return pl.pallas_call(
        functools.partial(pick_kernel, turn),
        out_shape=jax.ShapeDtypeStruct(own.shape, own.dtype),
        in_specs=[pl.BlockSpec(memory_space=pltpu.SMEM), vm, vm],
        out_specs=vm,
        compiler_params=pltpu.CompilerParams(vmem_limit_bytes=4 << 20),
        cost_estimate=pl.CostEstimate(flops=0, bytes_accessed=1 << 19, transcendentals=0),
        name="pick",
    )(ids, got, own)


def hidden_kernel(low, flat, high, h_ref):
    first, last = col_masks(C)

    def put(lanes, v):
        v = v.astype(F32)
        hid = v * (0.5 + 0.5 * jnp.tanh(0.5 * v))
        before, after = col_shifts(hid, first, last)
        h_ref[0, 0:C, lanes] = before.astype(BF16)
        h_ref[0, C:2 * C, lanes] = hid.astype(BF16)
        h_ref[0, 2 * C:3 * C, lanes] = after.astype(BF16)

    put(slice(0, W), low[0])
    put(slice(9 * W, 10 * W), high[0])

    @pl.loop(0, 8)
    def _(r):
        put(pl.ds(pl.multiple_of(r * W + W, W), W),
            flat[0, :, pl.ds(pl.multiple_of(r * W, W), W)])


def hidden_shifts(low, flat, high):
    spec = lambda n: pl.BlockSpec((1, C, n), lambda b: (b, 0, 0))
    return pl.pallas_call(
        hidden_kernel,
        grid=(2,),
        out_shape=jax.ShapeDtypeStruct((2, 3 * C, 10 * W), BF16),
        in_specs=[spec(W), spec(8 * W), spec(W)],
        out_specs=pl.BlockSpec((1, 3 * C, 10 * W), lambda b: (b, 0, 0)),
        compiler_params=pltpu.CompilerParams(vmem_limit_bytes=LIMIT),
        cost_estimate=pl.CostEstimate(
            flops=10 * 2 * C * 10 * W, bytes_accessed=6 << 20, transcendentals=2 * C * 10 * W),
        name="hidden",
    )(low, flat, high)


def wgrad_kernel(scale, ids, p0, p1, p2, p3, hid, keep, give, upper, sem):
    q = ids[0]
    core = ids[1]
    copies = []
    for d, ref in enumerate((p0, p1, p2, p3)):
        pos = q ^ d
        half = pl.multiple_of((pos & 1) * (BLK * W), BLK * W)
        copies.append(pltpu.make_async_copy(
            ref, upper.at[pos >> 1, :, pl.ds(half, BLK * W)], sem.at[d]))
    for copy in copies:
        copy.start()
    for copy in copies:
        copy.wait()
    @pl.loop(0, 3)
    def _(step):
        acc = None
        for b in range(2):
            term = lax.dot_general(
                upper[b], hid[b, :, pl.ds(pl.multiple_of(step * W, W), 8 * W)],
                (((1,), (1,)), ((), ())), preferred_element_type=F32)
            acc = term if acc is None else acc + term
        acc = (acc * scale).astype(BF16)
        for side in range(2):
            for owner, out in ((side, keep), (1 - side, give)):
                @pl.when(core == owner)
                def _(acc=acc, side=side, out=out):
                    for b in range(3):
                        for piece in range(8):
                            row = side * 128 + piece * 16
                            out[piece, 3 * step + b] = acc[row:row + 16, b * C:b * C + C]


def wgrad(scale, ids, parts, hid):
    hbm = pl.BlockSpec(memory_space=pl.ANY)
    return pl.pallas_call(
        functools.partial(wgrad_kernel, scale),
        out_shape=(jax.ShapeDtypeStruct((8, 9, 16, C), BF16),) * 2,
        in_specs=[pl.BlockSpec(memory_space=pltpu.SMEM)] + [hbm] * 4
        + [pl.BlockSpec(memory_space=pltpu.VMEM)],
        out_specs=(pl.BlockSpec(memory_space=pltpu.VMEM),) * 2,
        scratch_shapes=[
            pltpu.VMEM((2, C, 8 * W), BF16),
            pltpu.SemaphoreType.DMA((4,)),
        ],
        compiler_params=pltpu.CompilerParams(vmem_limit_bytes=LIMIT),
        cost_estimate=pl.CostEstimate(
            flops=2 * 9 * C * C * 2048, bytes_accessed=6 << 20, transcendentals=0),
        name="wgrad",
    )(ids, *parts, hid)


def place_kernel(ids, g0, g1, g2, g3, out):
    q = ids[0]
    for d, ref in enumerate((g0, g1, g2, g3)):
        pos = q ^ d
        half = pl.multiple_of((pos & 1) * (BLK * W), BLK * W)
        out[pos >> 1, :, pl.ds(half, BLK * W)] = ref[...]


def place(ids, parts):
    vm = pl.BlockSpec(memory_space=pltpu.VMEM)
    return pl.pallas_call(
        place_kernel,
        out_shape=jax.ShapeDtypeStruct((2, C, 8 * W), BF16),
        in_specs=[pl.BlockSpec(memory_space=pltpu.SMEM)] + [vm] * 4,
        out_specs=vm,
        cost_estimate=pl.CostEstimate(flops=0, bytes_accessed=2 << 20, transcendentals=0),
        compiler_params=pltpu.CompilerParams(vmem_limit_bytes=4 << 20),
        name="place",
    )(ids, *parts)


def unpack_kernel(ids, near, far, out):
    core = ids[1]
    for chip in range(8):
        for side, ref in ((core, near), (1 - core, far)):
            row = pl.multiple_of(side * 128 + chip * 16, 16)
            out[:, pl.ds(row, 16), :] = ref[chip].astype(F32)


def unpack(ids, near, far):
    vm = pl.BlockSpec(memory_space=pltpu.VMEM)
    return pl.pallas_call(
        unpack_kernel,
        out_shape=jax.ShapeDtypeStruct((9, C, C), F32),
        in_specs=[pl.BlockSpec(memory_space=pltpu.SMEM)] + [vm] * 2,
        out_specs=vm,
        cost_estimate=pl.CostEstimate(flops=0, bytes_accessed=4 << 20, transcendentals=0),
        compiler_params=pltpu.CompilerParams(vmem_limit_bytes=4 << 20),
        name="unpack",
    )(ids, near, far)


def per_device(acts, weights, cotangent):
    section = lax.axis_index(SECTION)
    tile = lax.axis_index(TILE)
    q = section & 3
    group = section >> 2
    core = tile & 1
    ids = jnp.stack([q, core, group]).astype(jnp.int32)
    n = BLK * W

    cot = lax.dynamic_slice(
        cotangent.reshape(2, C, 8 * W), (q >> 1, 0, (q & 1) * n), (1, C, n))[0]

    wt = weights[0].transpose(2, 0, 1).reshape(C, 9 * C)
    w_half = lax.dynamic_slice(wt, (core * 128, 0), (128, 9 * C))
    flat = acts[0].reshape(2, C, 8 * W)

    def piece_of(member):
        return lax.dynamic_slice(flat, (member >> 1, 0, (member & 1) * n), (1, C, n))[0]

    pieces = [piece_of(q ^ d) for d in range(4)]
    rims = (flat[:, :, 7 * W:], flat[:, :, :W])
    w_half, pieces, cot, rims, ids = lax.optimization_barrier((w_half, pieces, cot, rims, ids))
    near_y = swap_member(w_half, 1)
    near_z = swap_member(w_half, 2)
    pieces = [pieces[0]] + [swap_member(pieces[d], d) for d in (1, 2, 3)]
    near_y, near_z, pieces = lax.optimization_barrier((near_y, near_z, pieces))
    near_d = swap_member(near_y, 2)
    a_own, top, bottom = pack(ids, pieces)
    vup, vdn = from_above(bottom), from_below(top)
    top, bottom, cot = lax.optimization_barrier((top, bottom, cot))
    up, dn = from_above(cot), from_below(cot)
    near_d, vup, vdn, up, dn = lax.optimization_barrier((near_d, vup, vdn, up, dn))
    near = (near_y, near_z, near_d)
    slots = gather(ids, wt, *near, *[swap_core(block) for block in near])
    stored = (a_own, vup, vdn)

    own = last = cot
    for tick in range(4):
        if tick:
            got = send(last, lambda s, t: (s - 4, t) if s >> 2 == 4 - tick else None)
            own = pick(3 - tick, ids, got, own)
            up, dn = from_above(own), from_below(own)
        if tick == 1:
            low = send(rims[0], lambda s, t: (s, (t + 1) % 16))
            high = send(rims[1], lambda s, t: (s, (t - 1) % 16))
            hid = hidden_shifts(low, flat, high)
        if tick == 2:
            up, hid = lax.optimization_barrier((up, hid))
        last = chain(tick == 3, ids, up, own, dn, slots, stored)
    out_p, out_g = last

    parts = [out_p[0]] + [swap_member(out_p[d], d) for d in (1, 2, 3)]
    parts, out_g = lax.optimization_barrier((parts, out_g))
    grads = [out_g[0]] + [swap_member(out_g[d], d) for d in (1, 2, 3)]

    scale = 1.0 / (2 * 128 * 128) ** 0.5
    keep, give = wgrad(scale, ids, parts, hid)
    give, grads = lax.optimization_barrier((give, grads))
    both = (keep.astype(F32) + swap_core(give).astype(F32)).astype(BF16)
    pieces = lax.all_to_all(both, ("x", "yhi"), 0, 0, tiled=True)
    total = jnp.sum(pieces.astype(F32), axis=0).astype(BF16)
    copies = jnp.broadcast_to(total[None], (8,) + total.shape)
    gathered = lax.all_to_all(copies, ("x", "yhi"), 0, 0, tiled=True)
    weight_grad = unpack(ids, gathered, swap_core(gathered))

    grad_acts = place(ids, grads).reshape(1, 2, C, 8, W)
    return (grad_acts, weight_grad[None])


def solution(mesh):
    fine = Mesh(mesh.devices.reshape(16, 4, 2, 2), ("section", "x", "yhi", "core"))
    placed = (
        P(SECTION, None, None, TILE, None),
        P(SECTION, None, None, None),
        P(None, None, TILE, None),
    )
    return jax.shard_map(
        per_device,
        mesh=fine,
        in_specs=placed,
        out_specs=(P(SECTION, None, None, TILE, None), P(SECTION, None, None, None)),
        check_vma=False,
    )
```

```python
import functools

import jax
import jax.numpy as jnp
from jax import lax
from jax.experimental import pallas as pl
from jax.experimental.pallas import tpu as pltpu
from jax.sharding import Mesh, PartitionSpec as P

MEMBERS = ("zlo", "ylo")
SECTION = ("group",) + MEMBERS
TILE = ("x", "yhi", "core")
BOTH = SECTION + TILE
C = 256
W = 128
LIMIT = 16 << 20
BLK = 4
F32 = jnp.float32
BF16 = jnp.bfloat16


def route(target):
    pairs = []
    for s in range(16):
        for t in range(16):
            to = target(s, t)
            if to is not None:
                pairs.append((s * 16 + t, to[0] * 16 + to[1]))
    return pairs


def send(block, target):
    return lax.ppermute(block, BOTH, route(target))


def exchange(blocks):
    return lax.all_to_all(blocks, MEMBERS, 0, 0, tiled=True)


def swap_core(block):
    return send(block, lambda s, t: (s, t ^ 1))


def from_above(block):
    return send(block, lambda s, t: (s ^ 1, t if s & 1 == 0 else (t + 1) % 16))


def from_below(block):
    return send(block, lambda s, t: (s ^ 1, t if s & 1 == 1 else (t - 1) % 16))


def col_masks(rows):
    lane = lax.broadcasted_iota(jnp.int32, (rows, W), 1)
    return lane == 0, lane == W - 1


def col_shifts(x, first, last):
    before = jnp.where(first, 0.0, pltpu.roll(x, 1, 1))
    after = jnp.where(last, 0.0, pltpu.roll(x, W - 1, 1))
    return before, after


def pack_kernel(own, top, bottom):
    at = {3: 0, 2: 3, 1: 5}
    for layer in (1, 2, 3):
        lanes = slice(at[layer] * W, (at[layer] + layer) * W)
        top[:, lanes] = own[layer, :, :layer * W]
        bottom[:, lanes] = own[layer, :, (BLK - layer) * W:]


def pack(own):
    vm = pl.BlockSpec(memory_space=pltpu.VMEM)
    return pl.pallas_call(
        pack_kernel,
        out_shape=(jax.ShapeDtypeStruct((C, 6 * W), BF16),) * 2,
        in_specs=[vm],
        out_specs=(vm, vm),
        cost_estimate=pl.CostEstimate(flops=0, bytes_accessed=2 << 20, transcendentals=0),
        compiler_params=pltpu.CompilerParams(vmem_limit_bytes=4 << 20),
        name="pack",
    )(own)


def gather_kernel(ids, near, far, out, sem):
    mine = pl.multiple_of(ids[0] * 128, 128)
    other = pl.multiple_of((1 - ids[0]) * 128, 128)
    copies = [
        pltpu.make_async_copy(near, out.at[:, pl.ds(mine, 128)], sem.at[0]),
        pltpu.make_async_copy(far, out.at[:, pl.ds(other, 128)], sem.at[1]),
    ]
    for copy in copies:
        copy.start()
    for copy in copies:
        copy.wait()


def gather(ids, near, far):
    return pl.pallas_call(
        gather_kernel,
        out_shape=jax.ShapeDtypeStruct((4, C, 9 * C), BF16),
        in_specs=[pl.BlockSpec(memory_space=pltpu.SMEM)]
        + [pl.BlockSpec(memory_space=pl.ANY)] * 2,
        out_specs=pl.BlockSpec(memory_space=pltpu.VMEM),
        scratch_shapes=[pltpu.SemaphoreType.DMA((2,))],
        compiler_params=pltpu.CompilerParams(vmem_limit_bytes=4 << 20),
        cost_estimate=pl.CostEstimate(flops=0, bytes_accessed=9 << 20, transcendentals=0),
        name="gather",
    )(ids, near, far)


def chain_kernel(final, up, own, dn, wbuf, vown, vup, vdn, *refs):
    cat0, cat1 = refs[-2:]
    if final:
        out_p, out_g = refs[:2]
    else:
        out_last = refs[0]
    first, last = col_masks(C)

    def put(cat, row, x32):
        before, after = col_shifts(x32, first, last)
        lanes = slice(row * W, row * W + W)
        cat[0:C, lanes] = after.astype(BF16)
        cat[C:2 * C, lanes] = x32.astype(BF16)
        cat[2 * C:3 * C, lanes] = before.astype(BF16)

    for part, ref in enumerate((up, own, dn)):
        for r in range(BLK):
            put(cat0, part * BLK + r, ref[:, r * W:r * W + W].astype(F32))

    at = {3: 0, 2: 3, 1: 5}

    def stored_row(layer, r):
        if r < layer:
            ref, row = vup, at[layer] + r
        elif r < layer + BLK:
            return vown[layer, :, (r - layer) * W:(r - layer + 1) * W].astype(F32)
        else:
            ref, row = vdn, at[layer] + r - layer - BLK
        return ref[:, row * W:row * W + W].astype(F32)

    cats = (cat0, cat1)
    for j in range(4):
        layer = 3 - j
        cur, nxt = cats[j % 2], cats[(j + 1) % 2]
        rows_out = 10 - 2 * j
        if final:
            out_p[layer] = cur[C:2 * C, (4 - j) * W:(8 - j) * W]
        for ch in range(rows_out // 2):
            back = None
            for a in (-1, 0, 1):
                start = (1 - a + 2 * ch) * W
                term = jnp.dot(
                    wbuf[layer, :, 768 * (a + 1):768 * (a + 2)],
                    cur[:, start:start + 2 * W],
                    preferred_element_type=F32,
                )
                back = term if back is None else back + term
            for r in (2 * ch, 2 * ch + 1):
                v = stored_row(layer, r)
                sig = 0.5 + 0.5 * jnp.tanh(0.5 * v)
                slope = sig * (1.0 + v * (1.0 - sig))
                mid = cur[C:2 * C, (1 + r) * W:(2 + r) * W].astype(F32)
                new = mid + back[:, (r - 2 * ch) * W:(r - 2 * ch + 1) * W] * slope
                if j < 3:
                    put(nxt, r, new)
                elif final:
                    out_g[layer, :, r * W:r * W + W] = new.astype(BF16)
                else:
                    out_last[:, r * W:r * W + W] = new.astype(BF16)
        if final and j < 3:
            out_g[layer] = nxt[C:2 * C, (3 - j) * W:(7 - j) * W]


def chain(final, up, own, dn, weights, stored):
    vm = pl.BlockSpec(memory_space=pltpu.VMEM)
    n = BLK * W
    if final:
        out_shape = (jax.ShapeDtypeStruct((4, C, n), BF16),) * 2
    else:
        out_shape = jax.ShapeDtypeStruct((C, n), BF16)
    return pl.pallas_call(
        functools.partial(chain_kernel, final),
        out_shape=out_shape,
        in_specs=[vm] * 7,
        out_specs=(vm, vm) if final else vm,
        scratch_shapes=[
            pltpu.VMEM((3 * C, 12 * W), BF16),
            pltpu.VMEM((3 * C, 12 * W), BF16),
        ],
        compiler_params=pltpu.CompilerParams(vmem_limit_bytes=LIMIT),
        cost_estimate=pl.CostEstimate(
            flops=2 * 9 * C * C * 28 * W, bytes_accessed=10 << 20, transcendentals=28 * W * C),
        name="chain",
    )(up, own, dn, weights, *stored)


def pick_kernel(turn, ids, got, own, out):
    out[...] = jnp.where(ids[1] == turn, got[...], own[...])


def pick(turn, ids, got, own):
    vm = pl.BlockSpec(memory_space=pltpu.VMEM)
    return pl.pallas_call(
        functools.partial(pick_kernel, turn),
        out_shape=jax.ShapeDtypeStruct(own.shape, own.dtype),
        in_specs=[pl.BlockSpec(memory_space=pltpu.SMEM), vm, vm],
        out_specs=vm,
        compiler_params=pltpu.CompilerParams(vmem_limit_bytes=4 << 20),
        cost_estimate=pl.CostEstimate(flops=0, bytes_accessed=1 << 19, transcendentals=0),
        name="pick",
    )(ids, got, own)


def hidden_kernel(low, flat, high, h_ref):
    first, last = col_masks(C)

    def put(lanes, v):
        v = v.astype(F32)
        hid = v * (0.5 + 0.5 * jnp.tanh(0.5 * v))
        before, after = col_shifts(hid, first, last)
        h_ref[0, 0:C, lanes] = before.astype(BF16)
        h_ref[0, C:2 * C, lanes] = hid.astype(BF16)
        h_ref[0, 2 * C:3 * C, lanes] = after.astype(BF16)

    put(slice(0, W), low[0])
    put(slice(9 * W, 10 * W), high[0])

    @pl.loop(0, 8)
    def _(r):
        put(pl.ds(pl.multiple_of(r * W + W, W), W),
            flat[0, :, pl.ds(pl.multiple_of(r * W, W), W)])


def hidden_shifts(low, flat, high):
    spec = lambda n: pl.BlockSpec((1, C, n), lambda b: (b, 0, 0))
    return pl.pallas_call(
        hidden_kernel,
        grid=(2,),
        out_shape=jax.ShapeDtypeStruct((2, 3 * C, 10 * W), BF16),
        in_specs=[spec(W), spec(8 * W), spec(W)],
        out_specs=pl.BlockSpec((1, 3 * C, 10 * W), lambda b: (b, 0, 0)),
        compiler_params=pltpu.CompilerParams(vmem_limit_bytes=LIMIT),
        cost_estimate=pl.CostEstimate(
            flops=10 * 2 * C * 10 * W, bytes_accessed=6 << 20, transcendentals=2 * C * 10 * W),
        name="hidden",
    )(low, flat, high)


def wgrad_kernel(scale, ids, parts, h_hbm, keep, give, upper, hid, sem):
    core = ids[0]
    copies = [pltpu.make_async_copy(h_hbm.at[b], hid.at[b], sem.at[4 + b]) for b in range(2)]
    for pos in range(4):
        lanes = slice((pos & 1) * BLK * W, ((pos & 1) + 1) * BLK * W)
        copies.append(pltpu.make_async_copy(
            parts.at[pos], upper.at[pos >> 1, :, lanes], sem.at[pos]))
    for copy in copies:
        copy.start()
    for copy in copies:
        copy.wait()

    @pl.loop(0, 3)
    def _(step):
        acc = None
        for b in range(2):
            term = lax.dot_general(
                upper[b], hid[b, :, pl.ds(pl.multiple_of(step * W, W), 8 * W)],
                (((1,), (1,)), ((), ())), preferred_element_type=F32)
            acc = term if acc is None else acc + term
        acc = (acc * scale).astype(BF16)
        for side in range(2):
            for owner, out in ((side, keep), (1 - side, give)):
                @pl.when(core == owner)
                def _(acc=acc, side=side, out=out):
                    for b in range(3):
                        for piece in range(8):
                            row = side * 128 + piece * 16
                            out[piece, 3 * step + b] = acc[row:row + 16, b * C:b * C + C]


def wgrad(scale, ids, parts, hid):
    hbm = pl.BlockSpec(memory_space=pl.ANY)
    return pl.pallas_call(
        functools.partial(wgrad_kernel, scale),
        out_shape=(jax.ShapeDtypeStruct((8, 9, 16, C), BF16),) * 2,
        in_specs=[pl.BlockSpec(memory_space=pltpu.SMEM), hbm, hbm],
        out_specs=(pl.BlockSpec(memory_space=pltpu.VMEM),) * 2,
        scratch_shapes=[
            pltpu.VMEM((2, C, 8 * W), BF16),
            pltpu.VMEM((2, 3 * C, 10 * W), BF16),
            pltpu.SemaphoreType.DMA((6,)),
        ],
        compiler_params=pltpu.CompilerParams(vmem_limit_bytes=LIMIT),
        cost_estimate=pl.CostEstimate(
            flops=2 * 9 * C * C * 2048, bytes_accessed=6 << 20, transcendentals=0),
        name="wgrad",
    )(ids, parts, pltpu.with_memory_space_constraint(hid, pltpu.HBM))


def place_kernel(parts, out):
    for pos in range(4):
        out[pos >> 1, :, (pos & 1) * BLK * W:((pos & 1) + 1) * BLK * W] = parts[pos]


def place(parts):
    vm = pl.BlockSpec(memory_space=pltpu.VMEM)
    return pl.pallas_call(
        place_kernel,
        out_shape=jax.ShapeDtypeStruct((2, C, 8 * W), BF16),
        in_specs=[vm],
        out_specs=vm,
        cost_estimate=pl.CostEstimate(flops=0, bytes_accessed=2 << 20, transcendentals=0),
        compiler_params=pltpu.CompilerParams(vmem_limit_bytes=4 << 20),
        name="place",
    )(parts)


def unpack_kernel(ids, near, far, out):
    core = ids[0]
    for chip in range(8):
        for side, ref in ((core, near), (1 - core, far)):
            row = pl.multiple_of(side * 128 + chip * 16, 16)
            out[:, pl.ds(row, 16), :] = ref[chip].astype(F32)


def unpack(ids, near, far):
    vm = pl.BlockSpec(memory_space=pltpu.VMEM)
    return pl.pallas_call(
        unpack_kernel,
        out_shape=jax.ShapeDtypeStruct((9, C, C), F32),
        in_specs=[pl.BlockSpec(memory_space=pltpu.SMEM)] + [vm] * 2,
        out_specs=vm,
        cost_estimate=pl.CostEstimate(flops=0, bytes_accessed=4 << 20, transcendentals=0),
        compiler_params=pltpu.CompilerParams(vmem_limit_bytes=4 << 20),
        name="unpack",
    )(ids, near, far)


def per_device(acts, weights, cotangent):
    section = lax.axis_index(SECTION)
    tile = lax.axis_index(TILE)
    q = section & 3
    core = tile & 1
    ids = jnp.stack([core, section >> 2]).astype(jnp.int32)
    n = BLK * W

    cot = lax.dynamic_slice(
        cotangent.reshape(2, C, 8 * W), (q >> 1, 0, (q & 1) * n), (1, C, n))[0]

    wt = weights[0].transpose(2, 0, 1).reshape(C, 9 * C)
    w_half = lax.dynamic_slice(wt, (core * 128, 0), (128, 9 * C))
    w_all = jnp.broadcast_to(w_half[None], (4, 128, 9 * C))
    flat = acts[0].reshape(2, C, 8 * W)
    pieces = jnp.stack([flat[m >> 1, :, (m & 1) * n:(m & 1) * n + n] for m in range(4)])
    rims = (flat[:, :, 7 * W:], flat[:, :, :W])
    w_all, pieces, cot, rims, ids = lax.optimization_barrier((w_all, pieces, cot, rims, ids))
    a_own = exchange(pieces)
    top, bottom = pack(a_own)
    w_all, top, bottom, cot = lax.optimization_barrier((w_all, top, bottom, cot))
    vup, vdn = from_above(bottom), from_below(top)
    up, dn = from_above(cot), from_below(cot)
    near = exchange(w_all)
    near, vup, vdn, up, dn = lax.optimization_barrier((near, vup, vdn, up, dn))
    stored = (a_own, vup, vdn)
    slots = gather(ids, near, swap_core(near))

    own = last = cot
    for tick in range(4):
        if tick:
            got = send(last, lambda s, t: (s - 4, t) if s >> 2 == 4 - tick else None)
            own = pick(3 - tick, ids, got, own)
            up, dn = from_above(own), from_below(own)
        if tick == 1:
            low = send(rims[0], lambda s, t: (s, (t + 1) % 16))
            high = send(rims[1], lambda s, t: (s, (t - 1) % 16))
            hid = hidden_shifts(low, flat, high)
        if tick == 2:
            up, hid = lax.optimization_barrier((up, hid))
        last = chain(tick == 3, up, own, dn, slots, stored)
    out_p, out_g = last

    parts = exchange(out_p)
    parts, out_g = lax.optimization_barrier((parts, out_g))
    grads = exchange(out_g)

    scale = 1.0 / (2 * 128 * 128) ** 0.5
    keep, give = wgrad(scale, ids, parts, hid)
    give, grads = lax.optimization_barrier((give, grads))
    both = (keep.astype(F32) + swap_core(give).astype(F32)).astype(BF16)
    pieces = lax.all_to_all(both, ("x", "yhi"), 0, 0, tiled=True)
    total = jnp.sum(pieces.astype(F32), axis=0).astype(BF16)
    copies = jnp.broadcast_to(total[None], (8,) + total.shape)
    gathered = lax.all_to_all(copies, ("x", "yhi"), 0, 0, tiled=True)
    weight_grad = unpack(ids, gathered, swap_core(gathered))

    grad_acts = place(grads).reshape(1, 2, C, 8, W)
    return (grad_acts, weight_grad[None])


def solution(mesh):
    fine = Mesh(mesh.devices.reshape(4, 2, 2, 4, 2, 2), BOTH)
    placed = (
        P(SECTION, None, None, TILE, None),
        P(SECTION, None, None, None),
        P(None, None, TILE, None),
    )
    return jax.shard_map(
        per_device,
        mesh=fine,
        in_specs=placed,
        out_specs=(P(SECTION, None, None, TILE, None), P(SECTION, None, None, None)),
        check_vma=False,
    )
```

```python
import functools

import jax
import jax.numpy as jnp
from jax import lax
from jax.experimental import pallas as pl
from jax.experimental.pallas import tpu as pltpu
from jax.sharding import Mesh, PartitionSpec as P

SECTION = "section"
TILE = ("x", "yhi", "core")
BOTH = (SECTION,) + TILE
C = 256
W = 128
LIMIT = 16 << 20
BLK = 4
F32 = jnp.float32
BF16 = jnp.bfloat16


def route(target):
    pairs = []
    for s in range(16):
        for t in range(16):
            to = target(s, t)
            if to is not None:
                pairs.append((s * 16 + t, to[0] * 16 + to[1]))
    return pairs


def send(block, target):
    return lax.ppermute(block, BOTH, route(target))


def swap_member(block, d):
    return send(block, lambda s, t: (s ^ d, t))


def swap_core(block):
    return send(block, lambda s, t: (s, t ^ 1))


def from_above(block):
    return send(block, lambda s, t: (s ^ 1, t if s & 1 == 0 else (t + 1) % 16))


def from_below(block):
    return send(block, lambda s, t: (s ^ 1, t if s & 1 == 1 else (t - 1) % 16))


def col_masks(rows):
    lane = lax.broadcasted_iota(jnp.int32, (rows, W), 1)
    return lane == 0, lane == W - 1


def col_shifts(x, first, last):
    before = jnp.where(first, 0.0, pltpu.roll(x, 1, 1))
    after = jnp.where(last, 0.0, pltpu.roll(x, W - 1, 1))
    return before, after


def pack_kernel(ids, p0, p1, p2, p3, own, top, bottom):
    q = ids[0]
    at = {3: 0, 2: 3, 1: 5}
    for layer in range(4):
        for d, ref in enumerate((p0, p1, p2, p3)):
            @pl.when((q ^ d) == layer)
            def _(layer=layer, ref=ref):
                own[layer] = ref[...]
                if layer:
                    lanes = slice(at[layer] * W, (at[layer] + layer) * W)
                    top[:, lanes] = ref[:, :layer * W]
                    bottom[:, lanes] = ref[:, (BLK - layer) * W:]


def pack(ids, pieces):
    vm = pl.BlockSpec(memory_space=pltpu.VMEM)
    return pl.pallas_call(
        pack_kernel,
        out_shape=(
            jax.ShapeDtypeStruct((4, C, BLK * W), BF16),
            jax.ShapeDtypeStruct((C, 6 * W), BF16),
            jax.ShapeDtypeStruct((C, 6 * W), BF16),
        ),
        in_specs=[pl.BlockSpec(memory_space=pltpu.SMEM)] + [vm] * 4,
        out_specs=(vm, vm, vm),
        cost_estimate=pl.CostEstimate(flops=0, bytes_accessed=3 << 20, transcendentals=0),
        compiler_params=pltpu.CompilerParams(vmem_limit_bytes=4 << 20),
        name="pack",
    )(ids, *pieces)


def gather_kernel(ids, w0, r1, r2, r3, c1, c2, c3, out, sem):
    core = ids[1]
    mine = pl.multiple_of(core * 128, 128)
    other = pl.multiple_of((1 - core) * 128, 128)
    q = ids[0]
    copies = [pltpu.make_async_copy(w0, out.at[q], sem.at[0])]
    for d, (near, far) in enumerate(((r1, c1), (r2, c2), (r3, c3)), 1):
        copies += [
            pltpu.make_async_copy(near, out.at[q ^ d, pl.ds(mine, 128)], sem.at[d]),
            pltpu.make_async_copy(far, out.at[q ^ d, pl.ds(other, 128)], sem.at[3 + d]),
        ]
    for copy in copies:
        copy.start()
    for copy in copies:
        copy.wait()


def gather(ids, *blocks):
    return pl.pallas_call(
        gather_kernel,
        out_shape=jax.ShapeDtypeStruct((4, C, 9 * C), BF16),
        in_specs=[pl.BlockSpec(memory_space=pltpu.SMEM)]
        + [pl.BlockSpec(memory_space=pl.ANY)] * 7,
        out_specs=pl.BlockSpec(memory_space=pltpu.VMEM),
        scratch_shapes=[pltpu.SemaphoreType.DMA((7,))],
        compiler_params=pltpu.CompilerParams(vmem_limit_bytes=4 << 20),
        cost_estimate=pl.CostEstimate(flops=0, bytes_accessed=9 << 20, transcendentals=0),
        name="gather",
    )(ids, *blocks)


def chain_kernel(final, ids, up, own, dn, wbuf, vown, vup, vdn, *refs):
    q = ids[0]
    cat0, cat1 = refs[-2:]
    if final:
        out_p, out_g = refs[:2]
    else:
        out_last = refs[0]
    first, last = col_masks(C)

    def put(cat, row, x32):
        before, after = col_shifts(x32, first, last)
        lanes = slice(row * W, row * W + W)
        cat[0:C, lanes] = after.astype(BF16)
        cat[C:2 * C, lanes] = x32.astype(BF16)
        cat[2 * C:3 * C, lanes] = before.astype(BF16)

    for part, ref in enumerate((up, own, dn)):
        for r in range(BLK):
            put(cat0, part * BLK + r, ref[:, r * W:r * W + W].astype(F32))

    at = {3: 0, 2: 3, 1: 5}

    def stored_row(layer, r):
        if r < layer:
            ref, row = vup, at[layer] + r
        elif r < layer + BLK:
            return vown[layer, :, (r - layer) * W:(r - layer + 1) * W].astype(F32)
        else:
            ref, row = vdn, at[layer] + r - layer - BLK
        return ref[:, row * W:row * W + W].astype(F32)

    cats = (cat0, cat1)
    for j in range(4):
        layer = 3 - j
        slot = q ^ layer
        cur, nxt = cats[j % 2], cats[(j + 1) % 2]
        rows_out = 10 - 2 * j
        if final:
            out_p[slot] = cur[C:2 * C, (4 - j) * W:(8 - j) * W]
        for ch in range(rows_out // 2):
            back = None
            for a in (-1, 0, 1):
                start = (1 - a + 2 * ch) * W
                term = jnp.dot(
                    wbuf[layer, :, 768 * (a + 1):768 * (a + 2)],
                    cur[:, start:start + 2 * W],
                    preferred_element_type=F32,
                )
                back = term if back is None else back + term
            for r in (2 * ch, 2 * ch + 1):
                v = stored_row(layer, r)
                sig = 0.5 + 0.5 * jnp.tanh(0.5 * v)
                slope = sig * (1.0 + v * (1.0 - sig))
                mid = cur[C:2 * C, (1 + r) * W:(2 + r) * W].astype(F32)
                new = mid + back[:, (r - 2 * ch) * W:(r - 2 * ch + 1) * W] * slope
                if j < 3:
                    put(nxt, r, new)
                elif final:
                    out_g[slot, :, r * W:r * W + W] = new.astype(BF16)
                else:
                    out_last[:, r * W:r * W + W] = new.astype(BF16)
        if final and j < 3:
            out_g[slot] = nxt[C:2 * C, (3 - j) * W:(7 - j) * W]


def chain(final, ids, up, own, dn, weights, stored):
    vm = pl.BlockSpec(memory_space=pltpu.VMEM)
    n = BLK * W
    if final:
        out_shape = (jax.ShapeDtypeStruct((4, C, n), BF16),) * 2
    else:
        out_shape = jax.ShapeDtypeStruct((C, n), BF16)
    return pl.pallas_call(
        functools.partial(chain_kernel, final),
        out_shape=out_shape,
        in_specs=[pl.BlockSpec(memory_space=pltpu.SMEM)] + [vm] * 7,
        out_specs=(vm, vm) if final else vm,
        scratch_shapes=[
            pltpu.VMEM((3 * C, 12 * W), BF16),
            pltpu.VMEM((3 * C, 12 * W), BF16),
        ],
        compiler_params=pltpu.CompilerParams(vmem_limit_bytes=LIMIT),
        cost_estimate=pl.CostEstimate(
            flops=2 * 9 * C * C * 28 * W, bytes_accessed=10 << 20, transcendentals=28 * W * C),
        name="chain",
    )(ids, up, own, dn, weights, *stored)


def pick_kernel(turn, ids, got, own, out):
    out[...] = jnp.where(ids[2] == turn, got[...], own[...])


def pick(turn, ids, got, own):
    vm = pl.BlockSpec(memory_space=pltpu.VMEM)
    return pl.pallas_call(
        functools.partial(pick_kernel, turn),
        out_shape=jax.ShapeDtypeStruct(own.shape, own.dtype),
        in_specs=[pl.BlockSpec(memory_space=pltpu.SMEM), vm, vm],
        out_specs=vm,
        compiler_params=pltpu.CompilerParams(vmem_limit_bytes=4 << 20),
        cost_estimate=pl.CostEstimate(flops=0, bytes_accessed=1 << 19, transcendentals=0),
        name="pick",
    )(ids, got, own)


def order_kernel(ids, far, side, up, dn):
    upper_half = (ids[0] & 1) == 0
    up[...] = jnp.where(upper_half, far[...], side[...])
    dn[...] = jnp.where(upper_half, side[...], far[...])


def order(ids, far, side):
    vm = pl.BlockSpec(memory_space=pltpu.VMEM)
    return pl.pallas_call(
        order_kernel,
        out_shape=(jax.ShapeDtypeStruct(far.shape, far.dtype),) * 2,
        in_specs=[pl.BlockSpec(memory_space=pltpu.SMEM), vm, vm],
        out_specs=(vm, vm),
        compiler_params=pltpu.CompilerParams(vmem_limit_bytes=4 << 20),
        cost_estimate=pl.CostEstimate(flops=0, bytes_accessed=1 << 20, transcendentals=0),
        name="order",
    )(ids, far, side)


def hidden_kernel(low, flat, high, h_ref):
    first, last = col_masks(C)

    def put(lanes, v):
        v = v.astype(F32)
        hid = v * (0.5 + 0.5 * jnp.tanh(0.5 * v))
        before, after = col_shifts(hid, first, last)
        h_ref[0, 0:C, lanes] = before.astype(BF16)
        h_ref[0, C:2 * C, lanes] = hid.astype(BF16)
        h_ref[0, 2 * C:3 * C, lanes] = after.astype(BF16)

    put(slice(0, W), low[0])
    put(slice(9 * W, 10 * W), high[0])

    @pl.loop(0, 8)
    def _(r):
        put(pl.ds(pl.multiple_of(r * W + W, W), W),
            flat[0, :, pl.ds(pl.multiple_of(r * W, W), W)])


def hidden_shifts(low, flat, high):
    spec = lambda n: pl.BlockSpec((1, C, n), lambda b: (b, 0, 0))
    return pl.pallas_call(
        hidden_kernel,
        grid=(2,),
        out_shape=jax.ShapeDtypeStruct((2, 3 * C, 10 * W), BF16),
        in_specs=[spec(W), spec(8 * W), spec(W)],
        out_specs=pl.BlockSpec((1, 3 * C, 10 * W), lambda b: (b, 0, 0)),
        compiler_params=pltpu.CompilerParams(vmem_limit_bytes=LIMIT),
        cost_estimate=pl.CostEstimate(
            flops=10 * 2 * C * 10 * W, bytes_accessed=6 << 20, transcendentals=2 * C * 10 * W),
        name="hidden",
    )(low, flat, high)


def wgrad_kernel(scale, ids, p0, p1, p2, p3, hid, keep, give, upper, sem):
    q = ids[0]
    core = ids[1]
    copies = []
    for d, ref in enumerate((p0, p1, p2, p3)):
        pos = q ^ d
        half = pl.multiple_of((pos & 1) * (BLK * W), BLK * W)
        copies.append(pltpu.make_async_copy(
            ref, upper.at[pos >> 1, :, pl.ds(half, BLK * W)], sem.at[d]))
    for copy in copies:
        copy.start()
    for copy in copies:
        copy.wait()
    @pl.loop(0, 3)
    def _(step):
        acc = None
        for b in range(2):
            term = lax.dot_general(
                upper[b], hid[b, :, pl.ds(pl.multiple_of(step * W, W), 8 * W)],
                (((1,), (1,)), ((), ())), preferred_element_type=F32)
            acc = term if acc is None else acc + term
        acc = (acc * scale).astype(BF16)
        for side in range(2):
            for owner, out in ((side, keep), (1 - side, give)):
                @pl.when(core == owner)
                def _(acc=acc, side=side, out=out):
                    for b in range(3):
                        for piece in range(8):
                            row = side * 128 + piece * 16
                            out[piece, 3 * step + b] = acc[row:row + 16, b * C:b * C + C]


def wgrad(scale, ids, parts, hid):
    hbm = pl.BlockSpec(memory_space=pl.ANY)
    return pl.pallas_call(
        functools.partial(wgrad_kernel, scale),
        out_shape=(jax.ShapeDtypeStruct((8, 9, 16, C), BF16),) * 2,
        in_specs=[pl.BlockSpec(memory_space=pltpu.SMEM)] + [hbm] * 4
        + [pl.BlockSpec(memory_space=pltpu.VMEM)],
        out_specs=(pl.BlockSpec(memory_space=pltpu.VMEM),) * 2,
        scratch_shapes=[
            pltpu.VMEM((2, C, 8 * W), BF16),
            pltpu.SemaphoreType.DMA((4,)),
        ],
        compiler_params=pltpu.CompilerParams(vmem_limit_bytes=LIMIT),
        cost_estimate=pl.CostEstimate(
            flops=2 * 9 * C * C * 2048, bytes_accessed=6 << 20, transcendentals=0),
        name="wgrad",
    )(ids, *parts, hid)


def place_kernel(ids, g0, g1, g2, g3, out):
    q = ids[0]
    for d, ref in enumerate((g0, g1, g2, g3)):
        pos = q ^ d
        half = pl.multiple_of((pos & 1) * (BLK * W), BLK * W)
        out[pos >> 1, :, pl.ds(half, BLK * W)] = ref[...]


def place(ids, parts):
    vm = pl.BlockSpec(memory_space=pltpu.VMEM)
    return pl.pallas_call(
        place_kernel,
        out_shape=jax.ShapeDtypeStruct((2, C, 8 * W), BF16),
        in_specs=[pl.BlockSpec(memory_space=pltpu.SMEM)] + [vm] * 4,
        out_specs=vm,
        cost_estimate=pl.CostEstimate(flops=0, bytes_accessed=2 << 20, transcendentals=0),
        compiler_params=pltpu.CompilerParams(vmem_limit_bytes=4 << 20),
        name="place",
    )(ids, *parts)


def unpack_kernel(ids, near, far, out):
    core = ids[1]
    for chip in range(8):
        for side, ref in ((core, near), (1 - core, far)):
            row = pl.multiple_of(side * 128 + chip * 16, 16)
            out[:, pl.ds(row, 16), :] = ref[chip].astype(F32)


def unpack(ids, near, far):
    vm = pl.BlockSpec(memory_space=pltpu.VMEM)
    return pl.pallas_call(
        unpack_kernel,
        out_shape=jax.ShapeDtypeStruct((9, C, C), F32),
        in_specs=[pl.BlockSpec(memory_space=pltpu.SMEM)] + [vm] * 2,
        out_specs=vm,
        cost_estimate=pl.CostEstimate(flops=0, bytes_accessed=4 << 20, transcendentals=0),
        compiler_params=pltpu.CompilerParams(vmem_limit_bytes=4 << 20),
        name="unpack",
    )(ids, near, far)


def per_device(acts, weights, cotangent):
    section = lax.axis_index(SECTION)
    tile = lax.axis_index(TILE)
    q = section & 3
    group = section >> 2
    core = tile & 1
    ids = jnp.stack([q, core, group]).astype(jnp.int32)
    n = BLK * W

    cots = cotangent.reshape(2, C, 8 * W)
    cot = lax.dynamic_slice(cots, (q >> 1, 0, (q & 1) * n), (1, C, n))[0]
    cot_side = lax.dynamic_slice(cots, (q >> 1, 0, (1 - (q & 1)) * n), (1, C, n))[0]

    wt = weights[0].transpose(2, 0, 1).reshape(C, 9 * C)
    w_half = lax.dynamic_slice(wt, (core * 128, 0), (128, 9 * C))
    flat = acts[0].reshape(2, C, 8 * W)

    def piece_of(member):
        return lax.dynamic_slice(flat, (member >> 1, 0, (member & 1) * n), (1, C, n))[0]

    pieces = [piece_of(q ^ d) for d in range(4)]
    rims = (flat[:, :, 7 * W:], flat[:, :, :W])
    w_half, pieces, cot, cot_side, rims, ids = lax.optimization_barrier(
        (w_half, pieces, cot, cot_side, rims, ids))
    near_y = swap_member(w_half, 1)
    near_z = swap_member(w_half, 2)
    pieces = [pieces[0]] + [swap_member(pieces[d], d) for d in (1, 2, 3)]
    near_y, near_z, pieces, cot_side = lax.optimization_barrier((near_y, near_z, pieces, cot_side))
    near_d = swap_member(near_y, 2)
    cot_far = send(cot_side, lambda s, t: (s, (t + 1 if s & 1 == 0 else t - 1) % 16))
    a_own, top, bottom = pack(ids, pieces)
    vup, vdn = from_above(bottom), from_below(top)
    up, dn = order(ids, cot_far, cot_side)
    near_d, vup, vdn, up, dn = lax.optimization_barrier((near_d, vup, vdn, up, dn))
    near = (near_y, near_z, near_d)
    slots = gather(ids, wt, *near, *[swap_core(block) for block in near])
    stored = (a_own, vup, vdn)

    own = last = cot
    for tick in range(4):
        if tick:
            got = send(last, lambda s, t: (s - 4, t) if s >> 2 == 4 - tick else None)
            own = pick(3 - tick, ids, got, own)
            up, dn = from_above(own), from_below(own)
        if tick == 1:
            low = send(rims[0], lambda s, t: (s, (t + 1) % 16))
            high = send(rims[1], lambda s, t: (s, (t - 1) % 16))
            hid = hidden_shifts(low, flat, high)
        if tick == 2:
            up, hid = lax.optimization_barrier((up, hid))
        last = chain(tick == 3, ids, up, own, dn, slots, stored)
    out_p, out_g = last

    parts = [out_p[0]] + [swap_member(out_p[d], d) for d in (1, 2, 3)]
    parts, out_g = lax.optimization_barrier((parts, out_g))
    grads = [out_g[0]] + [swap_member(out_g[d], d) for d in (1, 2, 3)]

    scale = 1.0 / (2 * 128 * 128) ** 0.5
    keep, give = wgrad(scale, ids, parts, hid)
    give, grads = lax.optimization_barrier((give, grads))
    both = (keep.astype(F32) + swap_core(give).astype(F32)).astype(BF16)
    pieces = lax.all_to_all(both, ("x", "yhi"), 0, 0, tiled=True)
    total = jnp.sum(pieces.astype(F32), axis=0).astype(BF16)
    copies = jnp.broadcast_to(total[None], (8,) + total.shape)
    gathered = lax.all_to_all(copies, ("x", "yhi"), 0, 0, tiled=True)
    weight_grad = unpack(ids, gathered, swap_core(gathered))

    grad_acts = place(ids, grads).reshape(1, 2, C, 8, W)
    return (grad_acts, weight_grad[None])


def solution(mesh):
    fine = Mesh(mesh.devices.reshape(16, 4, 2, 2), ("section", "x", "yhi", "core"))
    placed = (
        P(SECTION, None, None, TILE, None),
        P(SECTION, None, None, None),
        P(None, None, TILE, None),
    )
    return jax.shard_map(
        per_device,
        mesh=fine,
        in_specs=placed,
        out_specs=(P(SECTION, None, None, TILE, None), P(SECTION, None, None, None)),
        check_vma=False,
    )
```

```python
import functools

import jax
import jax.numpy as jnp
from jax import lax
from jax.experimental import pallas as pl
from jax.experimental.pallas import tpu as pltpu
from jax.sharding import Mesh, PartitionSpec as P

SECTION = "section"
TILE = ("x", "yhi", "core")
BOTH = (SECTION,) + TILE
C = 256
W = 128
LIMIT = 16 << 20
BLK = 4
F32 = jnp.float32
BF16 = jnp.bfloat16


def route(target):
    pairs = []
    for s in range(16):
        for t in range(16):
            to = target(s, t)
            if to is not None:
                pairs.append((s * 16 + t, to[0] * 16 + to[1]))
    return pairs


def send(block, target):
    return lax.ppermute(block, BOTH, route(target))


def swap_member(block, d):
    return send(block, lambda s, t: (s ^ d, t))


def swap_core(block):
    return send(block, lambda s, t: (s, t ^ 1))


def from_above(block):
    return send(block, lambda s, t: (s ^ 1, t if s & 1 == 0 else (t + 1) % 16))


def from_below(block):
    return send(block, lambda s, t: (s ^ 1, t if s & 1 == 1 else (t - 1) % 16))


def col_masks(rows):
    lane = lax.broadcasted_iota(jnp.int32, (rows, W), 1)
    return lane == 0, lane == W - 1


def col_shifts(x, first, last):
    before = jnp.where(first, 0.0, pltpu.roll(x, 1, 1))
    after = jnp.where(last, 0.0, pltpu.roll(x, W - 1, 1))
    return before, after


def pack_kernel(ids, p0, p1, p2, p3, own, top, bottom):
    q = ids[0]
    at = {3: 0, 2: 3, 1: 5}
    for layer in range(4):
        for d, ref in enumerate((p0, p1, p2, p3)):
            @pl.when((q ^ d) == layer)
            def _(layer=layer, ref=ref):
                own[layer] = ref[...]
                if layer:
                    lanes = slice(at[layer] * W, (at[layer] + layer) * W)
                    top[:, lanes] = ref[:, :layer * W]
                    bottom[:, lanes] = ref[:, (BLK - layer) * W:]


def pack(ids, pieces):
    vm = pl.BlockSpec(memory_space=pltpu.VMEM)
    return pl.pallas_call(
        pack_kernel,
        out_shape=(
            jax.ShapeDtypeStruct((4, C, BLK * W), BF16),
            jax.ShapeDtypeStruct((C, 6 * W), BF16),
            jax.ShapeDtypeStruct((C, 6 * W), BF16),
        ),
        in_specs=[pl.BlockSpec(memory_space=pltpu.SMEM)] + [vm] * 4,
        out_specs=(vm, vm, vm),
        cost_estimate=pl.CostEstimate(flops=0, bytes_accessed=3 << 20, transcendentals=0),
        compiler_params=pltpu.CompilerParams(vmem_limit_bytes=4 << 20),
        name="pack",
    )(ids, *pieces)


def gather_kernel(ids, w0, r1, r2, r3, c1, c2, c3, out, sem):
    core = ids[1]
    mine = pl.multiple_of(core * 128, 128)
    other = pl.multiple_of((1 - core) * 128, 128)
    q = ids[0]
    copies = [pltpu.make_async_copy(w0, out.at[q], sem.at[0])]
    for d, (near, far) in enumerate(((r1, c1), (r2, c2), (r3, c3)), 1):
        copies += [
            pltpu.make_async_copy(near, out.at[q ^ d, pl.ds(mine, 128)], sem.at[d]),
            pltpu.make_async_copy(far, out.at[q ^ d, pl.ds(other, 128)], sem.at[3 + d]),
        ]
    for copy in copies:
        copy.start()
    for copy in copies:
        copy.wait()


def gather(ids, *blocks):
    return pl.pallas_call(
        gather_kernel,
        out_shape=jax.ShapeDtypeStruct((4, C, 9 * C), BF16),
        in_specs=[pl.BlockSpec(memory_space=pltpu.SMEM)]
        + [pl.BlockSpec(memory_space=pl.ANY)] * 7,
        out_specs=pl.BlockSpec(memory_space=pltpu.VMEM),
        scratch_shapes=[pltpu.SemaphoreType.DMA((7,))],
        compiler_params=pltpu.CompilerParams(vmem_limit_bytes=4 << 20),
        cost_estimate=pl.CostEstimate(flops=0, bytes_accessed=9 << 20, transcendentals=0),
        name="gather",
    )(ids, *blocks)


def chain_kernel(final, ids, up, own, dn, wbuf, vown, vup, vdn, *refs):
    q = ids[0]
    cat0, cat1 = refs[-2:]
    if final:
        out_p, out_g = refs[:2]
    else:
        out_last = refs[0]
    first, last = col_masks(C)

    def put(cat, row, x32):
        before, after = col_shifts(x32, first, last)
        lanes = slice(row * W, row * W + W)
        cat[0:C, lanes] = after.astype(BF16)
        cat[C:2 * C, lanes] = x32.astype(BF16)
        cat[2 * C:3 * C, lanes] = before.astype(BF16)

    for part, ref in enumerate((up, own, dn)):
        for r in range(BLK):
            put(cat0, part * BLK + r, ref[:, r * W:r * W + W].astype(F32))

    at = {3: 0, 2: 3, 1: 5}

    def stored_row(layer, r):
        if r < layer:
            ref, row = vup, at[layer] + r
        elif r < layer + BLK:
            return vown[layer, :, (r - layer) * W:(r - layer + 1) * W].astype(F32)
        else:
            ref, row = vdn, at[layer] + r - layer - BLK
        return ref[:, row * W:row * W + W].astype(F32)

    cats = (cat0, cat1)
    for j in range(4):
        layer = 3 - j
        slot = q ^ layer
        cur, nxt = cats[j % 2], cats[(j + 1) % 2]
        rows_out = 10 - 2 * j
        if final:
            out_p[slot] = cur[C:2 * C, (4 - j) * W:(8 - j) * W]
        for ch in range(rows_out // 2):
            back = None
            for a in (-1, 0, 1):
                start = (1 - a + 2 * ch) * W
                term = jnp.dot(
                    wbuf[layer, :, 768 * (a + 1):768 * (a + 2)],
                    cur[:, start:start + 2 * W],
                    preferred_element_type=F32,
                )
                back = term if back is None else back + term
            for r in (2 * ch, 2 * ch + 1):
                v = stored_row(layer, r)
                sig = 0.5 + 0.5 * jnp.tanh(0.5 * v)
                slope = sig * (1.0 + v * (1.0 - sig))
                mid = cur[C:2 * C, (1 + r) * W:(2 + r) * W].astype(F32)
                new = mid + back[:, (r - 2 * ch) * W:(r - 2 * ch + 1) * W] * slope
                if j < 3:
                    put(nxt, r, new)
                elif final:
                    out_g[slot, :, r * W:r * W + W] = new.astype(BF16)
                else:
                    out_last[:, r * W:r * W + W] = new.astype(BF16)
        if final and j < 3:
            out_g[slot] = nxt[C:2 * C, (3 - j) * W:(7 - j) * W]


def chain(final, ids, up, own, dn, weights, stored):
    vm = pl.BlockSpec(memory_space=pltpu.VMEM)
    n = BLK * W
    if final:
        out_shape = (jax.ShapeDtypeStruct((4, C, n), BF16),) * 2
    else:
        out_shape = jax.ShapeDtypeStruct((C, n), BF16)
    return pl.pallas_call(
        functools.partial(chain_kernel, final),
        out_shape=out_shape,
        in_specs=[pl.BlockSpec(memory_space=pltpu.SMEM)] + [vm] * 7,
        out_specs=(vm, vm) if final else vm,
        scratch_shapes=[
            pltpu.VMEM((3 * C, 12 * W), BF16),
            pltpu.VMEM((3 * C, 12 * W), BF16),
        ],
        compiler_params=pltpu.CompilerParams(vmem_limit_bytes=LIMIT),
        cost_estimate=pl.CostEstimate(
            flops=2 * 9 * C * C * 28 * W, bytes_accessed=10 << 20, transcendentals=28 * W * C),
        name="chain",
    )(ids, up, own, dn, weights, *stored)


def pick_kernel(turn, ids, got, own, out):
    out[...] = jnp.where(ids[2] == turn, got[...], own[...])


def pick(turn, ids, got, own):
    vm = pl.BlockSpec(memory_space=pltpu.VMEM)
    return pl.pallas_call(
        functools.partial(pick_kernel, turn),
        out_shape=jax.ShapeDtypeStruct(own.shape, own.dtype),
        in_specs=[pl.BlockSpec(memory_space=pltpu.SMEM), vm, vm],
        out_specs=vm,
        compiler_params=pltpu.CompilerParams(vmem_limit_bytes=4 << 20),
        cost_estimate=pl.CostEstimate(flops=0, bytes_accessed=1 << 19, transcendentals=0),
        name="pick",
    )(ids, got, own)


def order_kernel(ids, far, side, up, dn):
    upper_half = (ids[0] & 1) == 0
    up[...] = jnp.where(upper_half, far[...], side[...])
    dn[...] = jnp.where(upper_half, side[...], far[...])


def order(ids, far, side):
    vm = pl.BlockSpec(memory_space=pltpu.VMEM)
    return pl.pallas_call(
        order_kernel,
        out_shape=(jax.ShapeDtypeStruct(far.shape, far.dtype),) * 2,
        in_specs=[pl.BlockSpec(memory_space=pltpu.SMEM), vm, vm],
        out_specs=(vm, vm),
        compiler_params=pltpu.CompilerParams(vmem_limit_bytes=4 << 20),
        cost_estimate=pl.CostEstimate(flops=0, bytes_accessed=1 << 20, transcendentals=0),
        name="order",
    )(ids, far, side)


def hidden_kernel(low, flat, high, h_ref):
    first, last = col_masks(C)

    def put(lanes, v):
        v = v.astype(F32)
        hid = v * (0.5 + 0.5 * jnp.tanh(0.5 * v))
        before, after = col_shifts(hid, first, last)
        h_ref[0, 0:C, lanes] = before.astype(BF16)
        h_ref[0, C:2 * C, lanes] = hid.astype(BF16)
        h_ref[0, 2 * C:3 * C, lanes] = after.astype(BF16)

    put(slice(0, W), low[0])
    put(slice(9 * W, 10 * W), high[0])

    @pl.loop(0, 8)
    def _(r):
        put(pl.ds(pl.multiple_of(r * W + W, W), W),
            flat[0, :, pl.ds(pl.multiple_of(r * W, W), W)])


def hidden_shifts(low, flat, high):
    spec = lambda n: pl.BlockSpec((1, C, n), lambda b: (b, 0, 0))
    return pl.pallas_call(
        hidden_kernel,
        grid=(2,),
        out_shape=jax.ShapeDtypeStruct((2, 3 * C, 10 * W), BF16),
        in_specs=[spec(W), spec(8 * W), spec(W)],
        out_specs=pl.BlockSpec((1, 3 * C, 10 * W), lambda b: (b, 0, 0)),
        compiler_params=pltpu.CompilerParams(vmem_limit_bytes=LIMIT),
        cost_estimate=pl.CostEstimate(
            flops=10 * 2 * C * 10 * W, bytes_accessed=6 << 20, transcendentals=2 * C * 10 * W),
        name="hidden",
    )(low, flat, high)


def wgrad_kernel(scale, ids, p0, p1, p2, p3, hid, keep, give, upper, sem):
    q = ids[0]
    core = ids[1]
    copies = []
    for d, ref in enumerate((p0, p1, p2, p3)):
        pos = q ^ d
        half = pl.multiple_of((pos & 1) * (BLK * W), BLK * W)
        copies.append(pltpu.make_async_copy(
            ref, upper.at[pos >> 1, :, pl.ds(half, BLK * W)], sem.at[d]))
    for copy in copies:
        copy.start()
    for copy in copies:
        copy.wait()
    @pl.loop(0, 3)
    def _(step):
        acc = None
        for b in range(2):
            term = lax.dot_general(
                upper[b], hid[b, :, pl.ds(pl.multiple_of(step * W, W), 8 * W)],
                (((1,), (1,)), ((), ())), preferred_element_type=F32)
            acc = term if acc is None else acc + term
        acc = (acc * scale).astype(BF16)
        for side in range(2):
            for owner, out in ((side, keep), (1 - side, give)):
                @pl.when(core == owner)
                def _(acc=acc, side=side, out=out):
                    for b in range(3):
                        for piece in range(8):
                            row = side * 128 + piece * 16
                            out[piece, 3 * step + b] = acc[row:row + 16, b * C:b * C + C]


def wgrad(scale, ids, parts, hid):
    hbm = pl.BlockSpec(memory_space=pl.ANY)
    return pl.pallas_call(
        functools.partial(wgrad_kernel, scale),
        out_shape=(jax.ShapeDtypeStruct((8, 9, 16, C), BF16),) * 2,
        in_specs=[pl.BlockSpec(memory_space=pltpu.SMEM)] + [hbm] * 4
        + [pl.BlockSpec(memory_space=pltpu.VMEM)],
        out_specs=(pl.BlockSpec(memory_space=pltpu.VMEM),) * 2,
        scratch_shapes=[
            pltpu.VMEM((2, C, 8 * W), BF16),
            pltpu.SemaphoreType.DMA((4,)),
        ],
        compiler_params=pltpu.CompilerParams(vmem_limit_bytes=LIMIT),
        cost_estimate=pl.CostEstimate(
            flops=2 * 9 * C * C * 2048, bytes_accessed=6 << 20, transcendentals=0),
        name="wgrad",
    )(ids, *parts, hid)


def place_kernel(ids, g0, g1, g2, g3, out):
    q = ids[0]
    for d, ref in enumerate((g0, g1, g2, g3)):
        pos = q ^ d
        half = pl.multiple_of((pos & 1) * (BLK * W), BLK * W)
        out[pos >> 1, :, pl.ds(half, BLK * W)] = ref[...]


def place(ids, parts):
    vm = pl.BlockSpec(memory_space=pltpu.VMEM)
    return pl.pallas_call(
        place_kernel,
        out_shape=jax.ShapeDtypeStruct((2, C, 8 * W), BF16),
        in_specs=[pl.BlockSpec(memory_space=pltpu.SMEM)] + [vm] * 4,
        out_specs=vm,
        cost_estimate=pl.CostEstimate(flops=0, bytes_accessed=2 << 20, transcendentals=0),
        compiler_params=pltpu.CompilerParams(vmem_limit_bytes=4 << 20),
        name="place",
    )(ids, *parts)


def unpack_kernel(ids, near, far, out):
    core = ids[1]
    for chip in range(8):
        for side, ref in ((core, near), (1 - core, far)):
            row = pl.multiple_of(side * 128 + chip * 16, 16)
            out[:, pl.ds(row, 16), :] = ref[chip].astype(F32)


def unpack(ids, near, far):
    vm = pl.BlockSpec(memory_space=pltpu.VMEM)
    return pl.pallas_call(
        unpack_kernel,
        out_shape=jax.ShapeDtypeStruct((9, C, C), F32),
        in_specs=[pl.BlockSpec(memory_space=pltpu.SMEM)] + [vm] * 2,
        out_specs=vm,
        cost_estimate=pl.CostEstimate(flops=0, bytes_accessed=4 << 20, transcendentals=0),
        compiler_params=pltpu.CompilerParams(vmem_limit_bytes=4 << 20),
        name="unpack",
    )(ids, near, far)


def per_device(acts, weights, cotangent):
    section = lax.axis_index(SECTION)
    tile = lax.axis_index(TILE)
    q = section & 3
    group = section >> 2
    core = tile & 1
    ids = jnp.stack([q, core, group]).astype(jnp.int32)
    n = BLK * W

    cots = cotangent.reshape(2, C, 8 * W)
    cot = lax.dynamic_slice(cots, (q >> 1, 0, (q & 1) * n), (1, C, n))[0]
    cot_side = lax.dynamic_slice(cots, (q >> 1, 0, (1 - (q & 1)) * n), (1, C, n))[0]

    wt = weights[0].transpose(2, 0, 1).reshape(C, 9 * C)
    w_half = lax.dynamic_slice(wt, (core * 128, 0), (128, 9 * C))
    flat = acts[0].reshape(2, C, 8 * W)

    def piece_of(member):
        return lax.dynamic_slice(flat, (member >> 1, 0, (member & 1) * n), (1, C, n))[0]

    pieces = [piece_of(q ^ d) for d in range(4)]
    rims = (flat[:, :, 7 * W:], flat[:, :, :W])
    w_half, pieces, cot, cot_side, rims, ids = lax.optimization_barrier(
        (w_half, pieces, cot, cot_side, rims, ids))
    near_y = swap_member(w_half, 1)
    near_z = swap_member(w_half, 2)
    pieces = [pieces[0]] + [swap_member(pieces[d], d) for d in (1, 2, 3)]
    near_y, near_z, pieces, cot_side = lax.optimization_barrier((near_y, near_z, pieces, cot_side))
    near_d = swap_member(near_y, 2)
    cot_far = send(cot_side, lambda s, t: (s, (t + 1 if s & 1 == 0 else t - 1) % 16))
    a_own, top, bottom = pack(ids, pieces)
    vup, vdn = from_above(bottom), from_below(top)
    up, dn = order(ids, cot_far, cot_side)
    near_d, vup, vdn, up, dn = lax.optimization_barrier((near_d, vup, vdn, up, dn))
    near = (near_y, near_z, near_d)
    slots = gather(ids, wt, *near, *[swap_core(block) for block in near])
    stored = (a_own, vup, vdn)

    own = last = cot
    for tick in range(4):
        if tick:
            got = send(last, lambda s, t: (s - 4, t) if s >> 2 == 4 - tick else None)
            if tick == 1:
                low = send(rims[0], lambda s, t: (s, (t + 1) % 16))
                high = send(rims[1], lambda s, t: (s, (t - 1) % 16))
                hid = hidden_shifts(low, flat, high)
                got, hid = lax.optimization_barrier((got, hid))
            own = pick(3 - tick, ids, got, own)
            up, dn = from_above(own), from_below(own)
        last = chain(tick == 3, ids, up, own, dn, slots, stored)
    out_p, out_g = last

    parts = [out_p[0]] + [swap_member(out_p[d], d) for d in (1, 2, 3)]
    parts, out_g = lax.optimization_barrier((parts, out_g))
    grads = [out_g[0]] + [swap_member(out_g[d], d) for d in (1, 2, 3)]

    scale = 1.0 / (2 * 128 * 128) ** 0.5
    keep, give = wgrad(scale, ids, parts, hid)
    give, grads = lax.optimization_barrier((give, grads))
    both = (keep.astype(F32) + swap_core(give).astype(F32)).astype(BF16)
    pieces = lax.all_to_all(both, ("x", "yhi"), 0, 0, tiled=True)
    total = jnp.sum(pieces.astype(F32), axis=0).astype(BF16)
    copies = jnp.broadcast_to(total[None], (8,) + total.shape)
    gathered = lax.all_to_all(copies, ("x", "yhi"), 0, 0, tiled=True)
    weight_grad = unpack(ids, gathered, swap_core(gathered))

    grad_acts = place(ids, grads).reshape(1, 2, C, 8, W)
    return (grad_acts, weight_grad[None])


def solution(mesh):
    fine = Mesh(mesh.devices.reshape(16, 4, 2, 2), ("section", "x", "yhi", "core"))
    placed = (
        P(SECTION, None, None, TILE, None),
        P(SECTION, None, None, None),
        P(None, None, TILE, None),
    )
    return jax.shard_map(
        per_device,
        mesh=fine,
        in_specs=placed,
        out_specs=(P(SECTION, None, None, TILE, None), P(SECTION, None, None, None)),
        check_vma=False,
    )
```

```python
import functools

import jax
import jax.numpy as jnp
from jax import lax
from jax.experimental import pallas as pl
from jax.experimental.pallas import tpu as pltpu
from jax.sharding import Mesh, PartitionSpec as P

SECTION = "section"
TILE = ("x", "yhi", "core")
BOTH = (SECTION,) + TILE
C = 256
W = 128
LIMIT = 16 << 20
BLK = 4
F32 = jnp.float32
BF16 = jnp.bfloat16


def route(target):
    pairs = []
    for s in range(16):
        for t in range(16):
            to = target(s, t)
            if to is not None:
                pairs.append((s * 16 + t, to[0] * 16 + to[1]))
    return pairs


def send(block, target):
    return lax.ppermute(block, BOTH, route(target))


def swap_member(block, d):
    return send(block, lambda s, t: (s ^ d, t))


def swap_core(block):
    return send(block, lambda s, t: (s, t ^ 1))


def from_above(block):
    return send(block, lambda s, t: (s ^ 1, t if s & 1 == 0 else (t + 1) % 16))


def from_below(block):
    return send(block, lambda s, t: (s ^ 1, t if s & 1 == 1 else (t - 1) % 16))


def col_masks(rows):
    lane = lax.broadcasted_iota(jnp.int32, (rows, W), 1)
    return lane == 0, lane == W - 1


def col_shifts(x, first, last):
    before = jnp.where(first, 0.0, pltpu.roll(x, 1, 1))
    after = jnp.where(last, 0.0, pltpu.roll(x, W - 1, 1))
    return before, after


def pack_kernel(ids, p0, p1, p2, p3, own, top, bottom):
    q = ids[0]
    at = {3: 0, 2: 3, 1: 5}
    for layer in range(4):
        for d, ref in enumerate((p0, p1, p2, p3)):
            @pl.when((q ^ d) == layer)
            def _(layer=layer, ref=ref):
                own[layer] = ref[...]
                if layer:
                    lanes = slice(at[layer] * W, (at[layer] + layer) * W)
                    top[:, lanes] = ref[:, :layer * W]
                    bottom[:, lanes] = ref[:, (BLK - layer) * W:]


def pack(ids, pieces):
    vm = pl.BlockSpec(memory_space=pltpu.VMEM)
    return pl.pallas_call(
        pack_kernel,
        out_shape=(
            jax.ShapeDtypeStruct((4, C, BLK * W), BF16),
            jax.ShapeDtypeStruct((C, 6 * W), BF16),
            jax.ShapeDtypeStruct((C, 6 * W), BF16),
        ),
        in_specs=[pl.BlockSpec(memory_space=pltpu.SMEM)] + [vm] * 4,
        out_specs=(vm, vm, vm),
        cost_estimate=pl.CostEstimate(flops=0, bytes_accessed=3 << 20, transcendentals=0),
        compiler_params=pltpu.CompilerParams(vmem_limit_bytes=4 << 20),
        name="pack",
    )(ids, *pieces)


def gather_kernel(ids, w0, r1, r2, r3, c1, c2, c3, out, sem):
    core = ids[1]
    mine = pl.multiple_of(core * 128, 128)
    other = pl.multiple_of((1 - core) * 128, 128)
    q = ids[0]
    copies = [pltpu.make_async_copy(w0, out.at[q], sem.at[0])]
    for d, (near, far) in enumerate(((r1, c1), (r2, c2), (r3, c3)), 1):
        copies += [
            pltpu.make_async_copy(near, out.at[q ^ d, pl.ds(mine, 128)], sem.at[d]),
            pltpu.make_async_copy(far, out.at[q ^ d, pl.ds(other, 128)], sem.at[3 + d]),
        ]
    for copy in copies:
        copy.start()
    for copy in copies:
        copy.wait()


def gather(ids, *blocks):
    return pl.pallas_call(
        gather_kernel,
        out_shape=jax.ShapeDtypeStruct((4, C, 9 * C), BF16),
        in_specs=[pl.BlockSpec(memory_space=pltpu.SMEM)]
        + [pl.BlockSpec(memory_space=pl.ANY)] * 7,
        out_specs=pl.BlockSpec(memory_space=pltpu.VMEM),
        scratch_shapes=[pltpu.SemaphoreType.DMA((7,))],
        compiler_params=pltpu.CompilerParams(vmem_limit_bytes=4 << 20),
        cost_estimate=pl.CostEstimate(flops=0, bytes_accessed=9 << 20, transcendentals=0),
        name="gather",
    )(ids, *blocks)


def chain_kernel(final, ids, up, own, dn, wbuf, vown, vup, vdn, *refs):
    q = ids[0]
    cat0, cat1 = refs[-2:]
    if final:
        out_p, out_g = refs[:2]
    else:
        out_last = refs[0]
    first, last = col_masks(C)

    def put(cat, row, x32):
        before, after = col_shifts(x32, first, last)
        lanes = slice(row * W, row * W + W)
        cat[0:C, lanes] = after.astype(BF16)
        cat[C:2 * C, lanes] = x32.astype(BF16)
        cat[2 * C:3 * C, lanes] = before.astype(BF16)

    for part, ref in enumerate((up, own, dn)):
        for r in range(BLK):
            put(cat0, part * BLK + r, ref[:, r * W:r * W + W].astype(F32))

    at = {3: 0, 2: 3, 1: 5}

    def stored_row(layer, r):
        if r < layer:
            ref, row = vup, at[layer] + r
        elif r < layer + BLK:
            return vown[layer, :, (r - layer) * W:(r - layer + 1) * W].astype(F32)
        else:
            ref, row = vdn, at[layer] + r - layer - BLK
        return ref[:, row * W:row * W + W].astype(F32)

    cats = (cat0, cat1)
    for j in range(4):
        layer = 3 - j
        slot = q ^ layer
        cur, nxt = cats[j % 2], cats[(j + 1) % 2]
        rows_out = 10 - 2 * j
        if final:
            out_p[slot] = cur[C:2 * C, (4 - j) * W:(8 - j) * W]
        for ch in range(rows_out // 2):
            back = None
            for a in (-1, 0, 1):
                start = (1 - a + 2 * ch) * W
                term = jnp.dot(
                    wbuf[layer, :, 768 * (a + 1):768 * (a + 2)],
                    cur[:, start:start + 2 * W],
                    preferred_element_type=F32,
                )
                back = term if back is None else back + term
            for r in (2 * ch, 2 * ch + 1):
                v = stored_row(layer, r)
                sig = 0.5 + 0.5 * jnp.tanh(0.5 * v)
                slope = sig * (1.0 + v * (1.0 - sig))
                mid = cur[C:2 * C, (1 + r) * W:(2 + r) * W].astype(F32)
                new = mid + back[:, (r - 2 * ch) * W:(r - 2 * ch + 1) * W] * slope
                if j < 3:
                    put(nxt, r, new)
                elif final:
                    out_g[slot, :, r * W:r * W + W] = new.astype(BF16)
                else:
                    out_last[:, r * W:r * W + W] = new.astype(BF16)
        if final and j < 3:
            out_g[slot] = nxt[C:2 * C, (3 - j) * W:(7 - j) * W]


def chain(final, ids, up, own, dn, weights, stored):
    vm = pl.BlockSpec(memory_space=pltpu.VMEM)
    n = BLK * W
    if final:
        out_shape = (jax.ShapeDtypeStruct((4, C, n), BF16),) * 2
    else:
        out_shape = jax.ShapeDtypeStruct((C, n), BF16)
    return pl.pallas_call(
        functools.partial(chain_kernel, final),
        out_shape=out_shape,
        in_specs=[pl.BlockSpec(memory_space=pltpu.SMEM)] + [vm] * 7,
        out_specs=(vm, vm) if final else vm,
        scratch_shapes=[
            pltpu.VMEM((3 * C, 12 * W), BF16),
            pltpu.VMEM((3 * C, 12 * W), BF16),
        ],
        compiler_params=pltpu.CompilerParams(vmem_limit_bytes=LIMIT),
        cost_estimate=pl.CostEstimate(
            flops=2 * 9 * C * C * 28 * W, bytes_accessed=10 << 20, transcendentals=28 * W * C),
        name="chain",
    )(ids, up, own, dn, weights, *stored)


def pick_kernel(turn, ids, got, own, out):
    out[...] = jnp.where(ids[2] == turn, got[...], own[...])


def pick(turn, ids, got, own):
    vm = pl.BlockSpec(memory_space=pltpu.VMEM)
    return pl.pallas_call(
        functools.partial(pick_kernel, turn),
        out_shape=jax.ShapeDtypeStruct(own.shape, own.dtype),
        in_specs=[pl.BlockSpec(memory_space=pltpu.SMEM), vm, vm],
        out_specs=vm,
        compiler_params=pltpu.CompilerParams(vmem_limit_bytes=4 << 20),
        cost_estimate=pl.CostEstimate(flops=0, bytes_accessed=1 << 19, transcendentals=0),
        name="pick",
    )(ids, got, own)


def order_kernel(ids, far, side, up, dn):
    upper_half = (ids[0] & 1) == 0
    up[...] = jnp.where(upper_half, far[...], side[...])
    dn[...] = jnp.where(upper_half, side[...], far[...])


def order(ids, far, side):
    vm = pl.BlockSpec(memory_space=pltpu.VMEM)
    return pl.pallas_call(
        order_kernel,
        out_shape=(jax.ShapeDtypeStruct(far.shape, far.dtype),) * 2,
        in_specs=[pl.BlockSpec(memory_space=pltpu.SMEM), vm, vm],
        out_specs=(vm, vm),
        compiler_params=pltpu.CompilerParams(vmem_limit_bytes=4 << 20),
        cost_estimate=pl.CostEstimate(flops=0, bytes_accessed=1 << 20, transcendentals=0),
        name="order",
    )(ids, far, side)


def hidden_kernel(low, flat, high, h_ref):
    first, last = col_masks(C)

    def put(lanes, v):
        v = v.astype(F32)
        hid = v * (0.5 + 0.5 * jnp.tanh(0.5 * v))
        before, after = col_shifts(hid, first, last)
        h_ref[0, 0:C, lanes] = before.astype(BF16)
        h_ref[0, C:2 * C, lanes] = hid.astype(BF16)
        h_ref[0, 2 * C:3 * C, lanes] = after.astype(BF16)

    put(slice(0, W), low[0])
    put(slice(9 * W, 10 * W), high[0])

    @pl.loop(0, 8)
    def _(r):
        put(pl.ds(pl.multiple_of(r * W + W, W), W),
            flat[0, :, pl.ds(pl.multiple_of(r * W, W), W)])


def hidden_shifts(low, flat, high):
    spec = lambda n: pl.BlockSpec((1, C, n), lambda b: (b, 0, 0))
    return pl.pallas_call(
        hidden_kernel,
        grid=(2,),
        out_shape=jax.ShapeDtypeStruct((2, 3 * C, 10 * W), BF16),
        in_specs=[spec(W), spec(8 * W), spec(W)],
        out_specs=pl.BlockSpec((1, 3 * C, 10 * W), lambda b: (b, 0, 0)),
        compiler_params=pltpu.CompilerParams(vmem_limit_bytes=LIMIT),
        cost_estimate=pl.CostEstimate(
            flops=10 * 2 * C * 10 * W, bytes_accessed=6 << 20, transcendentals=2 * C * 10 * W),
        name="hidden",
    )(low, flat, high)


def wgrad_kernel(scale, ids, p0, p1, p2, p3, hid, keep, give, upper, sem):
    q = ids[0]
    core = ids[1]
    copies = []
    for d, ref in enumerate((p0, p1, p2, p3)):
        pos = q ^ d
        half = pl.multiple_of((pos & 1) * (BLK * W), BLK * W)
        copies.append(pltpu.make_async_copy(
            ref, upper.at[pos >> 1, :, pl.ds(half, BLK * W)], sem.at[d]))
    for copy in copies:
        copy.start()
    for copy in copies:
        copy.wait()
    @pl.loop(0, 3)
    def _(step):
        acc = None
        for b in range(2):
            term = lax.dot_general(
                upper[b], hid[b, :, pl.ds(pl.multiple_of(step * W, W), 8 * W)],
                (((1,), (1,)), ((), ())), preferred_element_type=F32)
            acc = term if acc is None else acc + term
        acc = (acc * scale).astype(BF16)
        for side in range(2):
            for owner, out in ((side, keep), (1 - side, give)):
                @pl.when(core == owner)
                def _(acc=acc, side=side, out=out):
                    for b in range(3):
                        for piece in range(8):
                            row = side * 128 + piece * 16
                            out[piece, 3 * step + b] = acc[row:row + 16, b * C:b * C + C]


def wgrad(scale, ids, parts, hid):
    hbm = pl.BlockSpec(memory_space=pl.ANY)
    return pl.pallas_call(
        functools.partial(wgrad_kernel, scale),
        out_shape=(jax.ShapeDtypeStruct((8, 9, 16, C), BF16),) * 2,
        in_specs=[pl.BlockSpec(memory_space=pltpu.SMEM)] + [hbm] * 4
        + [pl.BlockSpec(memory_space=pltpu.VMEM)],
        out_specs=(pl.BlockSpec(memory_space=pltpu.VMEM),) * 2,
        scratch_shapes=[
            pltpu.VMEM((2, C, 8 * W), BF16),
            pltpu.SemaphoreType.DMA((4,)),
        ],
        compiler_params=pltpu.CompilerParams(vmem_limit_bytes=LIMIT),
        cost_estimate=pl.CostEstimate(
            flops=2 * 9 * C * C * 2048, bytes_accessed=6 << 20, transcendentals=0),
        name="wgrad",
    )(ids, *parts, hid)


def place_kernel(ids, g0, g1, g2, g3, out):
    q = ids[0]
    for d, ref in enumerate((g0, g1, g2, g3)):
        pos = q ^ d
        half = pl.multiple_of((pos & 1) * (BLK * W), BLK * W)
        out[pos >> 1, :, pl.ds(half, BLK * W)] = ref[...]


def place(ids, parts):
    vm = pl.BlockSpec(memory_space=pltpu.VMEM)
    return pl.pallas_call(
        place_kernel,
        out_shape=jax.ShapeDtypeStruct((2, C, 8 * W), BF16),
        in_specs=[pl.BlockSpec(memory_space=pltpu.SMEM)] + [vm] * 4,
        out_specs=vm,
        cost_estimate=pl.CostEstimate(flops=0, bytes_accessed=2 << 20, transcendentals=0),
        compiler_params=pltpu.CompilerParams(vmem_limit_bytes=4 << 20),
        name="place",
    )(ids, *parts)


def unpack_kernel(ids, near, far, out):
    core = ids[1]
    for chip in range(8):
        for side, ref in ((core, near), (1 - core, far)):
            row = pl.multiple_of(side * 128 + chip * 16, 16)
            out[:, pl.ds(row, 16), :] = ref[chip].astype(F32)


def unpack(ids, near, far):
    vm = pl.BlockSpec(memory_space=pltpu.VMEM)
    return pl.pallas_call(
        unpack_kernel,
        out_shape=jax.ShapeDtypeStruct((9, C, C), F32),
        in_specs=[pl.BlockSpec(memory_space=pltpu.SMEM)] + [vm] * 2,
        out_specs=vm,
        cost_estimate=pl.CostEstimate(flops=0, bytes_accessed=4 << 20, transcendentals=0),
        compiler_params=pltpu.CompilerParams(vmem_limit_bytes=4 << 20),
        name="unpack",
    )(ids, near, far)


def per_device(acts, weights, cotangent):
    section = lax.axis_index(SECTION)
    tile = lax.axis_index(TILE)
    q = section & 3
    group = section >> 2
    core = tile & 1
    ids = jnp.stack([q, core, group]).astype(jnp.int32)
    n = BLK * W

    cots = cotangent.reshape(2, C, 8 * W)
    cot = lax.dynamic_slice(cots, (q >> 1, 0, (q & 1) * n), (1, C, n))[0]
    cot_side = lax.dynamic_slice(cots, (q >> 1, 0, (1 - (q & 1)) * n), (1, C, n))[0]

    wt = weights[0].transpose(2, 0, 1).reshape(C, 9 * C)
    w_half = lax.dynamic_slice(wt, (core * 128, 0), (128, 9 * C))
    flat = acts[0].reshape(2, C, 8 * W)

    def piece_of(member):
        return lax.dynamic_slice(flat, (member >> 1, 0, (member & 1) * n), (1, C, n))[0]

    pieces = [piece_of(q ^ d) for d in range(4)]
    rims = (flat[:, :, 7 * W:], flat[:, :, :W])
    pieces, cot, cot_side, rims, ids = lax.optimization_barrier(
        (pieces, cot, cot_side, rims, ids))
    near_y = swap_member(w_half, 1)
    near_z = swap_member(w_half, 2)
    pieces = [pieces[0]] + [swap_member(pieces[d], d) for d in (1, 2, 3)]
    near_y, near_z, pieces, cot_side = lax.optimization_barrier((near_y, near_z, pieces, cot_side))
    near_d = swap_member(near_y, 2)
    cot_far = send(cot_side, lambda s, t: (s, (t + 1 if s & 1 == 0 else t - 1) % 16))
    a_own, top, bottom = pack(ids, pieces)
    vup, vdn = from_above(bottom), from_below(top)
    up, dn = order(ids, cot_far, cot_side)
    near_d, vup, vdn, up, dn = lax.optimization_barrier((near_d, vup, vdn, up, dn))
    near = (near_y, near_z, near_d)
    slots = gather(ids, wt, *near, *[swap_core(block) for block in near])
    stored = (a_own, vup, vdn)

    own = last = cot
    for tick in range(4):
        if tick:
            got = send(last, lambda s, t: (s - 4, t) if s >> 2 == 4 - tick else None)
            if tick == 1:
                low = send(rims[0], lambda s, t: (s, (t + 1) % 16))
                high = send(rims[1], lambda s, t: (s, (t - 1) % 16))
                hid = hidden_shifts(low, flat, high)
                got, hid = lax.optimization_barrier((got, hid))
            own = pick(3 - tick, ids, got, own)
            up, dn = from_above(own), from_below(own)
        last = chain(tick == 3, ids, up, own, dn, slots, stored)
    out_p, out_g = last

    parts = [out_p[0]] + [swap_member(out_p[d], d) for d in (1, 2, 3)]
    parts, out_g = lax.optimization_barrier((parts, out_g))
    grads = [out_g[0]] + [swap_member(out_g[d], d) for d in (1, 2, 3)]

    scale = 1.0 / (2 * 128 * 128) ** 0.5
    keep, give = wgrad(scale, ids, parts, hid)
    give, grads = lax.optimization_barrier((give, grads))
    both = (keep.astype(F32) + swap_core(give).astype(F32)).astype(BF16)
    pieces = lax.all_to_all(both, ("x", "yhi"), 0, 0, tiled=True)
    total = jnp.sum(pieces.astype(F32), axis=0).astype(BF16)
    copies = jnp.broadcast_to(total[None], (8,) + total.shape)
    gathered = lax.all_to_all(copies, ("x", "yhi"), 0, 0, tiled=True)
    weight_grad = unpack(ids, gathered, swap_core(gathered))

    grad_acts = place(ids, grads).reshape(1, 2, C, 8, W)
    return (grad_acts, weight_grad[None])


def solution(mesh):
    fine = Mesh(mesh.devices.reshape(16, 4, 2, 2), ("section", "x", "yhi", "core"))
    placed = (
        P(SECTION, None, None, TILE, None),
        P(SECTION, None, None, None),
        P(None, None, TILE, None),
    )
    return jax.shard_map(
        per_device,
        mesh=fine,
        in_specs=placed,
        out_specs=(P(SECTION, None, None, TILE, None), P(SECTION, None, None, None)),
        check_vma=False,
    )
```

```python
import functools

import jax
import jax.numpy as jnp
from jax import lax
from jax.experimental import pallas as pl
from jax.experimental.pallas import tpu as pltpu
from jax.sharding import Mesh, PartitionSpec as P

SECTION = "section"
TILE = ("x", "yhi", "core")
BOTH = (SECTION,) + TILE
C = 256
W = 128
LIMIT = 16 << 20
BLK = 4
F32 = jnp.float32
BF16 = jnp.bfloat16


def route(target):
    pairs = []
    for s in range(16):
        for t in range(16):
            to = target(s, t)
            if to is not None:
                pairs.append((s * 16 + t, to[0] * 16 + to[1]))
    return pairs


def send(block, target):
    return lax.ppermute(block, BOTH, route(target))


def swap_member(block, d):
    return send(block, lambda s, t: (s ^ d, t))


def swap_core(block):
    return send(block, lambda s, t: (s, t ^ 1))


def from_above(block):
    return send(block, lambda s, t: (s ^ 1, t if s & 1 == 0 else (t + 1) % 16))


def from_below(block):
    return send(block, lambda s, t: (s ^ 1, t if s & 1 == 1 else (t - 1) % 16))


def col_masks(rows):
    lane = lax.broadcasted_iota(jnp.int32, (rows, W), 1)
    return lane == 0, lane == W - 1


def col_shifts(x, first, last):
    before = jnp.where(first, 0.0, pltpu.roll(x, 1, 1))
    after = jnp.where(last, 0.0, pltpu.roll(x, W - 1, 1))
    return before, after


def pack_kernel(ids, p0, p1, p2, p3, own, top, bottom):
    q = ids[0]
    at = {3: 0, 2: 3, 1: 5}
    for layer in range(4):
        for d, ref in enumerate((p0, p1, p2, p3)):
            @pl.when((q ^ d) == layer)
            def _(layer=layer, ref=ref):
                own[layer] = ref[...]
                if layer:
                    lanes = slice(at[layer] * W, (at[layer] + layer) * W)
                    top[:, lanes] = ref[:, :layer * W]
                    bottom[:, lanes] = ref[:, (BLK - layer) * W:]


def pack(ids, pieces):
    vm = pl.BlockSpec(memory_space=pltpu.VMEM)
    return pl.pallas_call(
        pack_kernel,
        out_shape=(
            jax.ShapeDtypeStruct((4, C, BLK * W), BF16),
            jax.ShapeDtypeStruct((C, 6 * W), BF16),
            jax.ShapeDtypeStruct((C, 6 * W), BF16),
        ),
        in_specs=[pl.BlockSpec(memory_space=pltpu.SMEM)] + [vm] * 4,
        out_specs=(vm, vm, vm),
        cost_estimate=pl.CostEstimate(flops=0, bytes_accessed=3 << 20, transcendentals=0),
        compiler_params=pltpu.CompilerParams(vmem_limit_bytes=4 << 20),
        name="pack",
    )(ids, *pieces)


def gather_kernel(ids, w0, r1, r2, r3, c1, c2, c3, out, sem):
    core = ids[1]
    mine = pl.multiple_of(core * 128, 128)
    other = pl.multiple_of((1 - core) * 128, 128)
    q = ids[0]
    copies = [pltpu.make_async_copy(w0, out.at[q], sem.at[0])]
    for d, (near, far) in enumerate(((r1, c1), (r2, c2), (r3, c3)), 1):
        copies += [
            pltpu.make_async_copy(near, out.at[q ^ d, pl.ds(mine, 128)], sem.at[d]),
            pltpu.make_async_copy(far, out.at[q ^ d, pl.ds(other, 128)], sem.at[3 + d]),
        ]
    for copy in copies:
        copy.start()
    for copy in copies:
        copy.wait()


def gather(ids, *blocks):
    return pl.pallas_call(
        gather_kernel,
        out_shape=jax.ShapeDtypeStruct((4, C, 9 * C), BF16),
        in_specs=[pl.BlockSpec(memory_space=pltpu.SMEM)]
        + [pl.BlockSpec(memory_space=pl.ANY)] * 7,
        out_specs=pl.BlockSpec(memory_space=pltpu.VMEM),
        scratch_shapes=[pltpu.SemaphoreType.DMA((7,))],
        compiler_params=pltpu.CompilerParams(vmem_limit_bytes=4 << 20),
        cost_estimate=pl.CostEstimate(flops=0, bytes_accessed=9 << 20, transcendentals=0),
        name="gather",
    )(ids, *blocks)


def chain_kernel(final, ids, up, own, dn, wbuf, vown, vup, vdn, *refs):
    q = ids[0]
    cat0, cat1 = refs[-2:]
    if final:
        out_p, out_g = refs[:2]
    else:
        out_last = refs[0]
    first, last = col_masks(C)

    def put(cat, row, x32):
        before, after = col_shifts(x32, first, last)
        lanes = slice(row * W, row * W + W)
        cat[0:C, lanes] = after.astype(BF16)
        cat[C:2 * C, lanes] = x32.astype(BF16)
        cat[2 * C:3 * C, lanes] = before.astype(BF16)

    for part, ref in enumerate((up, own, dn)):
        for r in range(BLK):
            put(cat0, part * BLK + r, ref[:, r * W:r * W + W].astype(F32))

    at = {3: 0, 2: 3, 1: 5}

    def stored_row(layer, r):
        if r < layer:
            ref, row = vup, at[layer] + r
        elif r < layer + BLK:
            return vown[layer, :, (r - layer) * W:(r - layer + 1) * W].astype(F32)
        else:
            ref, row = vdn, at[layer] + r - layer - BLK
        return ref[:, row * W:row * W + W].astype(F32)

    cats = (cat0, cat1)
    for j in range(4):
        layer = 3 - j
        slot = q ^ layer
        cur, nxt = cats[j % 2], cats[(j + 1) % 2]
        rows_out = 10 - 2 * j
        if final:
            out_p[slot] = cur[C:2 * C, (4 - j) * W:(8 - j) * W]
        for ch in range(rows_out // 2):
            back = None
            for a in (-1, 0, 1):
                start = (1 - a + 2 * ch) * W
                term = jnp.dot(
                    wbuf[layer, :, 768 * (a + 1):768 * (a + 2)],
                    cur[:, start:start + 2 * W],
                    preferred_element_type=F32,
                )
                back = term if back is None else back + term
            for r in (2 * ch, 2 * ch + 1):
                v = stored_row(layer, r)
                sig = 0.5 + 0.5 * jnp.tanh(0.5 * v)
                slope = sig * (1.0 + v * (1.0 - sig))
                mid = cur[C:2 * C, (1 + r) * W:(2 + r) * W].astype(F32)
                new = mid + back[:, (r - 2 * ch) * W:(r - 2 * ch + 1) * W] * slope
                if j < 3:
                    put(nxt, r, new)
                elif final:
                    out_g[slot, :, r * W:r * W + W] = new.astype(BF16)
                else:
                    out_last[:, r * W:r * W + W] = new.astype(BF16)
        if final and j < 3:
            out_g[slot] = nxt[C:2 * C, (3 - j) * W:(7 - j) * W]


def chain(final, ids, up, own, dn, weights, stored):
    vm = pl.BlockSpec(memory_space=pltpu.VMEM)
    n = BLK * W
    if final:
        out_shape = (jax.ShapeDtypeStruct((4, C, n), BF16),) * 2
    else:
        out_shape = jax.ShapeDtypeStruct((C, n), BF16)
    return pl.pallas_call(
        functools.partial(chain_kernel, final),
        out_shape=out_shape,
        in_specs=[pl.BlockSpec(memory_space=pltpu.SMEM)] + [vm] * 7,
        out_specs=(vm, vm) if final else vm,
        scratch_shapes=[
            pltpu.VMEM((3 * C, 12 * W), BF16),
            pltpu.VMEM((3 * C, 12 * W), BF16),
        ],
        compiler_params=pltpu.CompilerParams(vmem_limit_bytes=LIMIT),
        cost_estimate=pl.CostEstimate(
            flops=2 * 9 * C * C * 28 * W, bytes_accessed=10 << 20, transcendentals=28 * W * C),
        name="chain",
    )(ids, up, own, dn, weights, *stored)


def pick_kernel(turn, ids, got, own, out):
    out[...] = jnp.where(ids[2] == turn, got[...], own[...])


def pick(turn, ids, got, own):
    vm = pl.BlockSpec(memory_space=pltpu.VMEM)
    return pl.pallas_call(
        functools.partial(pick_kernel, turn),
        out_shape=jax.ShapeDtypeStruct(own.shape, own.dtype),
        in_specs=[pl.BlockSpec(memory_space=pltpu.SMEM), vm, vm],
        out_specs=vm,
        compiler_params=pltpu.CompilerParams(vmem_limit_bytes=4 << 20),
        cost_estimate=pl.CostEstimate(flops=0, bytes_accessed=1 << 19, transcendentals=0),
        name="pick",
    )(ids, got, own)


def order_kernel(ids, far, side, up, dn):
    upper_half = (ids[0] & 1) == 0
    up[...] = jnp.where(upper_half, far[...], side[...])
    dn[...] = jnp.where(upper_half, side[...], far[...])


def order(ids, far, side):
    vm = pl.BlockSpec(memory_space=pltpu.VMEM)
    return pl.pallas_call(
        order_kernel,
        out_shape=(jax.ShapeDtypeStruct(far.shape, far.dtype),) * 2,
        in_specs=[pl.BlockSpec(memory_space=pltpu.SMEM), vm, vm],
        out_specs=(vm, vm),
        compiler_params=pltpu.CompilerParams(vmem_limit_bytes=4 << 20),
        cost_estimate=pl.CostEstimate(flops=0, bytes_accessed=1 << 20, transcendentals=0),
        name="order",
    )(ids, far, side)


def hidden_kernel(low, flat, high, h_ref):
    first, last = col_masks(C)

    def put(lanes, v):
        v = v.astype(F32)
        hid = v * (0.5 + 0.5 * jnp.tanh(0.5 * v))
        before, after = col_shifts(hid, first, last)
        h_ref[0, 0:C, lanes] = before.astype(BF16)
        h_ref[0, C:2 * C, lanes] = hid.astype(BF16)
        h_ref[0, 2 * C:3 * C, lanes] = after.astype(BF16)

    put(slice(0, W), low[0])
    put(slice(9 * W, 10 * W), high[0])

    @pl.loop(0, 8)
    def _(r):
        put(pl.ds(pl.multiple_of(r * W + W, W), W),
            flat[0, :, pl.ds(pl.multiple_of(r * W, W), W)])


def hidden_shifts(low, flat, high):
    spec = lambda n: pl.BlockSpec((1, C, n), lambda b: (b, 0, 0))
    return pl.pallas_call(
        hidden_kernel,
        grid=(2,),
        out_shape=jax.ShapeDtypeStruct((2, 3 * C, 10 * W), BF16),
        in_specs=[spec(W), spec(8 * W), spec(W)],
        out_specs=pl.BlockSpec((1, 3 * C, 10 * W), lambda b: (b, 0, 0)),
        compiler_params=pltpu.CompilerParams(vmem_limit_bytes=LIMIT),
        cost_estimate=pl.CostEstimate(
            flops=10 * 2 * C * 10 * W, bytes_accessed=6 << 20, transcendentals=2 * C * 10 * W),
        name="hidden",
    )(low, flat, high)


def wgrad_kernel(scale, ids, p0, p1, p2, p3, hid, keep, give, upper, sem):
    q = ids[0]
    core = ids[1]
    copies = []
    for d, ref in enumerate((p0, p1, p2, p3)):
        pos = q ^ d
        half = pl.multiple_of((pos & 1) * (BLK * W), BLK * W)
        copies.append(pltpu.make_async_copy(
            ref, upper.at[pos >> 1, :, pl.ds(half, BLK * W)], sem.at[d]))
    for copy in copies:
        copy.start()
    for copy in copies:
        copy.wait()
    @pl.loop(0, 3)
    def _(step):
        acc = None
        for b in range(2):
            term = lax.dot_general(
                upper[b], hid[b, :, pl.ds(pl.multiple_of(step * W, W), 8 * W)],
                (((1,), (1,)), ((), ())), preferred_element_type=F32)
            acc = term if acc is None else acc + term
        acc = (acc * scale).astype(BF16)
        for side in range(2):
            for owner, out in ((side, keep), (1 - side, give)):
                @pl.when(core == owner)
                def _(acc=acc, side=side, out=out):
                    for b in range(3):
                        for piece in range(8):
                            row = side * 128 + piece * 16
                            out[piece, 3 * step + b] = acc[row:row + 16, b * C:b * C + C]


def wgrad(scale, ids, parts, hid):
    hbm = pl.BlockSpec(memory_space=pl.ANY)
    return pl.pallas_call(
        functools.partial(wgrad_kernel, scale),
        out_shape=(jax.ShapeDtypeStruct((8, 9, 16, C), BF16),) * 2,
        in_specs=[pl.BlockSpec(memory_space=pltpu.SMEM)] + [hbm] * 4
        + [pl.BlockSpec(memory_space=pltpu.VMEM)],
        out_specs=(pl.BlockSpec(memory_space=pltpu.VMEM),) * 2,
        scratch_shapes=[
            pltpu.VMEM((2, C, 8 * W), BF16),
            pltpu.SemaphoreType.DMA((4,)),
        ],
        compiler_params=pltpu.CompilerParams(vmem_limit_bytes=LIMIT),
        cost_estimate=pl.CostEstimate(
            flops=2 * 9 * C * C * 2048, bytes_accessed=6 << 20, transcendentals=0),
        name="wgrad",
    )(ids, *parts, hid)


def place_kernel(ids, g0, g1, g2, g3, out):
    q = ids[0]
    for d, ref in enumerate((g0, g1, g2, g3)):
        pos = q ^ d
        half = pl.multiple_of((pos & 1) * (BLK * W), BLK * W)
        out[pos >> 1, :, pl.ds(half, BLK * W)] = ref[...]


def place(ids, parts):
    vm = pl.BlockSpec(memory_space=pltpu.VMEM)
    return pl.pallas_call(
        place_kernel,
        out_shape=jax.ShapeDtypeStruct((2, C, 8 * W), BF16),
        in_specs=[pl.BlockSpec(memory_space=pltpu.SMEM)] + [vm] * 4,
        out_specs=vm,
        cost_estimate=pl.CostEstimate(flops=0, bytes_accessed=2 << 20, transcendentals=0),
        compiler_params=pltpu.CompilerParams(vmem_limit_bytes=4 << 20),
        name="place",
    )(ids, *parts)


def unpack_kernel(ids, near, far, out):
    core = ids[1]
    for chip in range(8):
        for side, ref in ((core, near), (1 - core, far)):
            row = pl.multiple_of(side * 128 + chip * 16, 16)
            out[:, pl.ds(row, 16), :] = ref[chip].astype(F32)


def unpack(ids, near, far):
    vm = pl.BlockSpec(memory_space=pltpu.VMEM)
    return pl.pallas_call(
        unpack_kernel,
        out_shape=jax.ShapeDtypeStruct((9, C, C), F32),
        in_specs=[pl.BlockSpec(memory_space=pltpu.SMEM)] + [vm] * 2,
        out_specs=vm,
        cost_estimate=pl.CostEstimate(flops=0, bytes_accessed=4 << 20, transcendentals=0),
        compiler_params=pltpu.CompilerParams(vmem_limit_bytes=4 << 20),
        name="unpack",
    )(ids, near, far)


def per_device(acts, weights, cotangent):
    section = lax.axis_index(SECTION)
    tile = lax.axis_index(TILE)
    q = section & 3
    group = section >> 2
    core = tile & 1
    ids = jnp.stack([q, core, group]).astype(jnp.int32)
    n = BLK * W

    cots = cotangent.reshape(2, C, 8 * W)
    cot = lax.dynamic_slice(cots, (q >> 1, 0, (q & 1) * n), (1, C, n))[0]
    cot_side = lax.dynamic_slice(cots, (q >> 1, 0, (1 - (q & 1)) * n), (1, C, n))[0]

    wt = weights[0].transpose(2, 0, 1).reshape(C, 9 * C)
    w_half = lax.dynamic_slice(weights[0], (0, 0, core * 128), (9, C, 128))
    w_half = w_half.transpose(2, 0, 1).reshape(128, 9 * C)
    flat = acts[0].reshape(2, C, 8 * W)

    def piece_of(member):
        return lax.dynamic_slice(flat, (member >> 1, 0, (member & 1) * n), (1, C, n))[0]

    pieces = [piece_of(q ^ d) for d in range(4)]
    rims = (flat[:, :, 7 * W:], flat[:, :, :W])
    pieces, cot, cot_side, rims, ids = lax.optimization_barrier(
        (pieces, cot, cot_side, rims, ids))
    near_y = swap_member(w_half, 1)
    near_z = swap_member(w_half, 2)
    pieces = [pieces[0]] + [swap_member(pieces[d], d) for d in (1, 2, 3)]
    near_y, near_z, pieces, cot_side = lax.optimization_barrier((near_y, near_z, pieces, cot_side))
    near_d = swap_member(near_y, 2)
    cot_far = send(cot_side, lambda s, t: (s, (t + 1 if s & 1 == 0 else t - 1) % 16))
    a_own, top, bottom = pack(ids, pieces)
    vup, vdn = from_above(bottom), from_below(top)
    up, dn = order(ids, cot_far, cot_side)
    near_d, vup, vdn, up, dn = lax.optimization_barrier((near_d, vup, vdn, up, dn))
    near = (near_y, near_z, near_d)
    slots = gather(ids, wt, *near, *[swap_core(block) for block in near])
    stored = (a_own, vup, vdn)

    own = last = cot
    for tick in range(4):
        if tick:
            got = send(last, lambda s, t: (s - 4, t) if s >> 2 == 4 - tick else None)
            if tick == 1:
                low = send(rims[0], lambda s, t: (s, (t + 1) % 16))
                high = send(rims[1], lambda s, t: (s, (t - 1) % 16))
                hid = hidden_shifts(low, flat, high)
                got, hid = lax.optimization_barrier((got, hid))
            own = pick(3 - tick, ids, got, own)
            up, dn = from_above(own), from_below(own)
        last = chain(tick == 3, ids, up, own, dn, slots, stored)
    out_p, out_g = last

    parts = [out_p[0]] + [swap_member(out_p[d], d) for d in (1, 2, 3)]
    parts, out_g = lax.optimization_barrier((parts, out_g))
    grads = [out_g[0]] + [swap_member(out_g[d], d) for d in (1, 2, 3)]

    scale = 1.0 / (2 * 128 * 128) ** 0.5
    keep, give = wgrad(scale, ids, parts, hid)
    give, grads = lax.optimization_barrier((give, grads))
    both = (keep.astype(F32) + swap_core(give).astype(F32)).astype(BF16)
    pieces = lax.all_to_all(both, ("x", "yhi"), 0, 0, tiled=True)
    total = jnp.sum(pieces.astype(F32), axis=0).astype(BF16)
    copies = jnp.broadcast_to(total[None], (8,) + total.shape)
    gathered = lax.all_to_all(copies, ("x", "yhi"), 0, 0, tiled=True)
    weight_grad = unpack(ids, gathered, swap_core(gathered))

    grad_acts = place(ids, grads).reshape(1, 2, C, 8, W)
    return (grad_acts, weight_grad[None])


def solution(mesh):
    fine = Mesh(mesh.devices.reshape(16, 4, 2, 2), ("section", "x", "yhi", "core"))
    placed = (
        P(SECTION, None, None, TILE, None),
        P(SECTION, None, None, None),
        P(None, None, TILE, None),
    )
    return jax.shard_map(
        per_device,
        mesh=fine,
        in_specs=placed,
        out_specs=(P(SECTION, None, None, TILE, None), P(SECTION, None, None, None)),
        check_vma=False,
    )
```
